32 devices in a mesh: fsdp: 8 (over z, x), head: 2 (over core), tensor: 2 (over y).
Axes of the slice: x: 2, y: 2, z: 4, core: 2. Of those that a mesh axis runs over, the one named last changes fastest.
Arguments:
- block_in: bfloat16 [4096, 1024], P('fsdp'), may hold values from -6 to 6
- cotangent: bfloat16 [4096, 1024], P('fsdp'), may hold values from -6 to 6
- norm_gain: float32 [1024], replicated, may hold values from 0.5 to 1.5
- w_x: bfloat16 [1024, 32, 64], P('fsdp', 'head', 'tensor'), may hold values from -0.1875 to 0.1875
- w_z: bfloat16 [1024, 32, 64], P('fsdp', 'head', 'tensor'), may hold values from -0.1875 to 0.1875
- w_bc: bfloat16 [1024, 2, 128], P('fsdp'), may hold values from -0.1875 to 0.1875
- w_dt: bfloat16 [1024, 32], P('fsdp', 'head'), may hold values from -0.1875 to 0.1875
- conv_x: float32 [32, 64, 4], P('head', 'tensor'), may hold values from -3 to 3
- conv_bc: float32 [2, 128, 4], replicated, may hold values from -3 to 3
- dt_bias: float32 [32], P('head'), may hold values from -6 to -2
- a_log: float32 [32], P('head'), may hold values from -1.5 to 0.5
- skip: float32 [32], P('head'), may hold values from 0.5 to 1.5
- gate_gain: float32 [32, 64], P('head', 'tensor'), may hold values from 0.5 to 1.5
- w_out: bfloat16 [32, 64, 1024], P('head', 'tensor', 'fsdp'), may hold values from -0.125 to 0.125
Outputs:
- block_out: bfloat16 [4096, 1024], P('fsdp')
- grad_in: float32 [4096, 1024], P('fsdp')
- grad_norm_gain: float32 [1024], replicated
- grad_w_x: float32 [1024, 32, 64], P('fsdp', 'head', 'tensor')
- grad_w_z: float32 [1024, 32, 64], P('fsdp', 'head', 'tensor')
- grad_w_bc: float32 [1024, 2, 128], P('fsdp')
- grad_w_dt: float32 [1024, 32], P('fsdp', 'head')
- grad_conv_x: float32 [32, 64, 4], P('head', 'tensor')
- grad_conv_bc: float32 [2, 128, 4], replicated
- grad_dt_bias: float32 [32], P('head')
- grad_a_log: float32 [32], P('head')
- grad_skip: float32 [32], P('head')
- grad_gate_gain: float32 [32, 64], P('head', 'tensor')
- grad_w_out: float32 [32, 64, 1024], P('head', 'tensor', 'fsdp')
The draws below stay inside these ranges and needn't reach their ends.
All inputs are finite; a program needn't handle non-finite values.
Results may differ from the reference program's by a relative error of at most 0.011.
Values may be sent and summed in bfloat16 or wider, within the bound.
A program may use at most 128 MiB of HBM per device.

```python
from functools import partial
import jax
import jax.numpy as jnp
from jax import lax

D = 1024
NH = 32
HD = 64
N = 128
K = 4
SPAN = 256
LEN = 512
DI = 2048
SEQS = 8
TOKENS = 4096


def raised(entries, stream_key, source, target, shards_of, factor):
    owner, partner = [(jnp.arange(entries.shape[axis_at]) // (entries.shape[axis_at] // shards_of)).reshape([-1 if axis == axis_at else 1 for axis in range(entries.ndim)]) for axis_at in (source, target)]
    chosen = jax.random.permutation(stream_key, shards_of)[partner]
    strong = (owner == chosen) | (owner == (partner + shards_of // 2) % shards_of)
    return jnp.where(strong, factor * entries, entries)


def level_of(stream_key, dims, pieces, low, top_value):
    gain = 1.0
    for axis_at, blocks in pieces:
        steps = jax.random.uniform(jax.random.fold_in(jax.random.fold_in(stream_key, 6), axis_at), (blocks,), jnp.float32, low / len(pieces), top_value / len(pieces))
        gain = gain * jnp.repeat(jnp.exp(steps), dims[axis_at] // blocks).reshape((-1,) + (1,) * (len(dims) - 1 - axis_at))
    return gain


def scatter_about(key, shape, scale, reach, pieces=(), dtype=jnp.bfloat16):
    drawn = jax.random.normal(key, shape, jnp.float32) * scale
    if len(pieces) > 0:
        drawn = level_of(key, shape, pieces, -0.22, 0.18) * drawn
    return jnp.clip(drawn, min=-reach, max=reach).astype(dtype)


def bell_draw_with(own_key, shape, width, limit, pieces, heavy, kind=jnp.bfloat16):
    entries = width * jax.random.normal(own_key, shape, jnp.float32)
    if pieces:
        entries = entries * level_of(own_key, shape, pieces, -0.22, 0.18)
    return jnp.clip(raised(entries, jax.random.fold_in(own_key, 3), *heavy), -limit, limit).astype(kind)


def setup_inputs(seed: int = 0) -> dict:
    key_of = jax.random.split(jax.random.key(seed), 15)
    block_in = bell_draw_with(key_of[0], (TOKENS, D), 1.0, 6.0, ((0, 8),), (0, 1, 8, 2.0))
    cotangent = bell_draw_with(key_of[1], (TOKENS, D), 1.0, 6.0, ((0, 8),), (0, 1, 8, 2.0))
    norm_gain = jnp.clip(1.0 + 0.1 * jax.random.normal(key_of[2], (D,), jnp.float32), 0.5, 1.5)
    w_x = scatter_about(key_of[3], (D, NH, HD), D ** -0.5, 0.1875, ((0, 8), (1, 2), (2, 2)))
    w_z = scatter_about(key_of[4], (D, NH, HD), D ** -0.5, 0.1875, ((0, 8), (1, 2), (2, 2)))
    w_bc = scatter_about(key_of[5], (D, 2, N), D ** -0.5, 0.1875, ((0, 8),))
    w_dt = scatter_about(key_of[6], (D, NH), D ** -0.5, 0.1875, ((0, 8), (1, 2)))
    conv_x = scatter_about(key_of[7], (NH, HD, K), K ** -0.5, 3.0, ((0, 2), (1, 2)), jnp.float32)
    conv_bc = scatter_about(key_of[8], (2, N, K), K ** -0.5, 3.0, (), jnp.float32)
    dt_bias = jnp.clip(-6.0 + 4.0 * jax.random.uniform(key_of[9], (NH,), jnp.float32) ** level_of(key_of[9], (NH,), ((0, 2),), -0.2, 0.2), -6.0, -2.0)
    a_log = jnp.clip(-1.5 + 2.0 * jax.random.uniform(key_of[10], (NH,), jnp.float32) ** level_of(key_of[10], (NH,), ((0, 2),), -0.2, 0.2), -1.5, 0.5)
    skip = jnp.clip(0.5 + 1.0 * jax.random.uniform(key_of[11], (NH,), jnp.float32) ** level_of(key_of[11], (NH,), ((0, 2),), -0.2, 0.2), 0.5, 1.5)
    gate_gain = jnp.clip(1.0 + 0.1 * jax.random.normal(key_of[12], (NH, HD), jnp.float32), 0.5, 1.5)
    w_out = scatter_about(key_of[13], (NH, HD, D), DI ** -0.5, 0.125, ((0, 2), (1, 2), (2, 8)))
    return {"block_in": block_in, "cotangent": cotangent, "norm_gain": norm_gain, "w_x": w_x, "w_z": w_z, "w_bc": w_bc, "w_dt": w_dt, "conv_x": conv_x, "conv_bc": conv_bc, "dt_bias": dt_bias, "a_log": a_log, "skip": skip, "gate_gain": gate_gain, "w_out": w_out}


EPSILON = 1e-05
PRECISE = lax.Precision.HIGHEST

def causal_conv(signal, kernel):
    taps = kernel.shape[1]
    length = signal.shape[0]
    padded = jnp.pad(signal, ((taps - 1, 0), (0, 0)))
    total = jnp.zeros_like(signal)
    for offset in range(taps):
        total = total + padded[offset:offset + length] * kernel[:, offset]
    return total

def conv_silu(signal, kernel):
    return jax.nn.silu(causal_conv(signal, kernel))

def silu_slope(value):
    sigma = jax.nn.sigmoid(value)
    return sigma * (1.0 + value * (1.0 - sigma))

def scan_spans(values, step_size, rate, b_maps, c_maps, block):
    length, head_count, channels = values.shape
    blocks = length // block
    logs = (step_size * rate).reshape(blocks, block, head_count)
    cums = jnp.cumsum(logs, axis=1)
    x_blocks = values.reshape(blocks, block, head_count, channels)
    dt_blocks = step_size.reshape(blocks, block, head_count)
    b_blocks = b_maps.reshape(blocks, block, -1)
    c_blocks = c_maps.reshape(blocks, block, -1)
    scores = jnp.einsum('cln,csn->cls', c_blocks, b_blocks, precision=PRECISE)
    causal = (jnp.arange(block)[:, None] >= jnp.arange(block)[None, :])[None, :, :, None]
    gaps = cums[:, :, None, :] - cums[:, None, :, :]
    decays = jnp.where(causal, jnp.exp(jnp.where(causal, gaps, 0.0)), 0.0)
    mixing = scores[..., None] * decays * dt_blocks[:, None, :, :]
    intra_part = jnp.einsum('clsh,cshp->clhp', mixing, x_blocks, precision=PRECISE)
    to_end = jnp.exp(cums[:, -1:, :] - cums) * dt_blocks
    states = jnp.einsum('csh,csn,cshp->chpn', to_end, b_blocks, x_blocks, precision=PRECISE)
    whole_decay = jnp.exp(cums[:, -1, :])
    carried = []
    running = jnp.zeros_like(states[0])
    for position in range(blocks):
        carried.append(running)
        running = running * whole_decay[position][:, None, None] + states[position]
    entering = jnp.stack(carried)
    inter_part = jnp.einsum('cln,clh,chpn->clhp', c_blocks, jnp.exp(cums), entering, precision=PRECISE)
    return (intra_part + inter_part).reshape(length, head_count, channels)

def mixer(values, dt_raw, dt_bias, a_log, skip, b_maps, c_maps, block):
    step_size = jax.nn.softplus(dt_raw + dt_bias)
    rate = -jnp.exp(a_log)
    return scan_spans(values, step_size, rate, b_maps, c_maps, block) + skip[:, None] * values

def one_sequence(params, rows_in, upstream_bf):
    norm_gain, w_x, w_z, w_bc, w_dt, conv_x, conv_bc, dt_bias, a_log, skip, gate_gain, w_out = params
    inner_width = NH * HD
    weight_x = w_x.reshape(D, inner_width)
    weight_z = w_z.reshape(D, inner_width)
    weight_bc = w_bc.reshape(D, 2 * N)
    weight_out = w_out.reshape(inner_width, D)
    kernel_x = conv_x.reshape(inner_width, K)
    kernel_bc = conv_bc.reshape(2 * N, K)
    gain_flat = gate_gain.reshape(inner_width)
    features = rows_in.astype(jnp.float32)
    scale_in = lax.rsqrt(lax.optimization_barrier(jnp.mean(features * features, axis=1, keepdims=True)) + EPSILON)
    normed = (features * scale_in * norm_gain).astype(jnp.bfloat16)
    x_raw = jnp.dot(normed, weight_x, preferred_element_type=jnp.float32)
    z_raw = jnp.dot(normed, weight_z, preferred_element_type=jnp.float32)
    bc_raw = jnp.dot(normed, weight_bc, preferred_element_type=jnp.float32)
    dt_raw = jnp.dot(normed, w_dt, preferred_element_type=jnp.float32)
    x_act = conv_silu(x_raw, kernel_x).astype(jnp.bfloat16)
    bc_act = conv_silu(bc_raw, kernel_bc).astype(jnp.bfloat16)
    values = x_act.astype(jnp.float32).reshape(LEN, NH, HD)
    b_maps = bc_act[:, :N].astype(jnp.float32)
    c_maps = bc_act[:, N:].astype(jnp.float32)
    mixed = mixer(values, dt_raw, dt_bias, a_log, skip, b_maps, c_maps, SPAN).reshape(LEN, inner_width)
    gated = mixed * jax.nn.silu(z_raw)
    scale_out = lax.rsqrt(lax.optimization_barrier(jnp.sum(gated * gated, axis=1, keepdims=True)) / inner_width + EPSILON)
    normed_out = (gated * scale_out * gain_flat).astype(jnp.bfloat16)
    block_out = (jnp.dot(normed_out, weight_out, preferred_element_type=jnp.float32) + features).astype(jnp.bfloat16)
    upstream = upstream_bf.astype(jnp.float32)
    d_normed_out = jnp.dot(upstream_bf, weight_out.T, preferred_element_type=jnp.float32)
    g_w_out = jnp.dot(normed_out.T, upstream_bf, preferred_element_type=jnp.float32)
    g_gate_gain = lax.optimization_barrier(jnp.sum(d_normed_out * gated * scale_out, axis=0))
    d_hat = d_normed_out * gain_flat
    inner_sum = lax.optimization_barrier(jnp.sum(d_hat * gated, axis=1, keepdims=True))
    d_gated = scale_out * d_hat - gated * scale_out ** 3 * inner_sum / inner_width
    d_mixed = d_gated * jax.nn.silu(z_raw)
    d_z = (d_gated * mixed * silu_slope(z_raw)).astype(jnp.bfloat16)
    _, pullback = jax.vjp(partial(mixer, block=SPAN), values, dt_raw, dt_bias, a_log, skip, b_maps, c_maps)
    d_xs, d_dt, g_dt_bias, g_a_log, g_skip, d_b, d_c = pullback(d_mixed.reshape(LEN, NH, HD))
    _, pull_x = jax.vjp(conv_silu, x_raw, kernel_x)
    d_x_raw, g_conv_x = pull_x(d_xs.reshape(LEN, inner_width))
    _, pull_bc = jax.vjp(conv_silu, bc_raw, kernel_bc)
    d_bc_raw, g_conv_bc = pull_bc(jnp.concatenate([d_b, d_c], axis=1))
    d_x_b = d_x_raw.astype(jnp.bfloat16)
    d_bc_b = d_bc_raw.astype(jnp.bfloat16)
    d_dt_b = d_dt.astype(jnp.bfloat16)
    g_w_x = jnp.dot(normed.T, d_x_b, preferred_element_type=jnp.float32)
    g_w_z = jnp.dot(normed.T, d_z, preferred_element_type=jnp.float32)
    g_w_bc = jnp.dot(normed.T, d_bc_b, preferred_element_type=jnp.float32)
    g_w_dt = jnp.dot(normed.T, d_dt_b, preferred_element_type=jnp.float32)
    d_normed = jnp.dot(d_x_b, weight_x.T, preferred_element_type=jnp.float32) + jnp.dot(d_z, weight_z.T, preferred_element_type=jnp.float32) + jnp.dot(d_dt_b, w_dt.T, preferred_element_type=jnp.float32) + jnp.dot(d_bc_b, weight_bc.T, preferred_element_type=jnp.float32)
    g_norm_gain = lax.optimization_barrier(jnp.sum(d_normed * features * scale_in, axis=0))
    d_in_hat = d_normed * norm_gain
    grad_in = scale_in * d_in_hat - features * scale_in ** 3 * lax.optimization_barrier(jnp.mean(d_in_hat * features, axis=1, keepdims=True)) + upstream
    grads = (g_norm_gain, g_w_x.reshape(D, NH, HD), g_w_z.reshape(D, NH, HD), g_w_bc.reshape(D, 2, N), g_w_dt, g_conv_x.reshape(NH, HD, K), g_conv_bc.reshape(2, N, K), g_dt_bias, g_a_log, g_skip, g_gate_gain.reshape(NH, HD), g_w_out.reshape(NH, HD, D))
    return (block_out, grad_in, grads)

def reference(block_in, cotangent, norm_gain, w_x, w_z, w_bc, w_dt, conv_x, conv_bc, dt_bias, a_log, skip, gate_gain, w_out):
    params = (norm_gain, w_x, w_z, w_bc, w_dt, conv_x, conv_bc, dt_bias, a_log, skip, gate_gain, w_out)
    start = tuple((jnp.zeros(leaf.shape, jnp.float32) for leaf in params))

    def step_fn(totals, pair):
        out_rows, grad_rows, grads = one_sequence(params, pair[0], pair[1])
        return (tuple((a + b for a, b in zip(totals, grads))), (out_rows, grad_rows))
    totals, stacked = lax.scan(step_fn, start, (block_in.reshape(SEQS, LEN, D), cotangent.reshape(SEQS, LEN, D)))
    block_out = stacked[0].reshape(TOKENS, D)
    grad_in = stacked[1].reshape(TOKENS, D)
    return (block_out, grad_in, totals[0], totals[1], totals[2], totals[3], totals[4], totals[5], totals[6], totals[7], totals[8], totals[9], totals[10], totals[11])
```

```python
from functools import partial

import jax
import jax.numpy as jnp
from jax import lax
from jax.experimental import pallas as pl
from jax.experimental.pallas import tpu as pltpu
from jax.sharding import PartitionSpec as P

EPSILON = 1e-05
PRECISE = lax.Precision.HIGHEST
LANES = 128
CHUNK = 256
MESH = pl.DeviceIdType.MESH
VMEM_SPEC = pl.BlockSpec(memory_space=pltpu.VMEM)


def ring_index(position, count):
    high = position // (count // 2)
    return (1 - high) * 2 * position + high * (2 * (count - 1 - position) + 1)


def ring_position(index, count):
    odd = index % 2
    return (1 - odd) * (index // 2) + odd * (count - 1 - index // 2)


def ring_setup(count):
    me = lax.axis_index("fsdp")
    position = ring_position(me, count)
    right = ring_index((position + 1) % count, count)
    left = ring_index((position + count - 1) % count, count)
    barrier = pltpu.get_barrier_semaphore()
    for neighbour in (left, right):
        pl.semaphore_signal(barrier, inc=1, device_id={"fsdp": neighbour}, device_id_type=MESH)
    pl.semaphore_wait(barrier, 2)
    return me, position, (right, left)


def gather_kernel(count, split, x_ref, o_ref, local_sem, send_sem, recv_sem):
    me, position, targets = ring_setup(count)
    local = pltpu.make_async_copy(x_ref, o_ref.at[me], local_sem)
    local.start()
    width = x_ref.shape[1]
    columns = (pl.ds(0, split), pl.ds(split, width - split))
    copies = [[], []]
    for step in range(count - 1):
        for way in (0, 1):
            shift = count - step if way == 0 else step
            block = ring_index((position + shift) % count, count)
            target = o_ref.at[block, :, columns[way]]
            source = x_ref.at[:, columns[way]] if step == 0 else target
            if step > 0:
                copies[way][step - 1].wait_recv()
            copy = pltpu.make_async_remote_copy(
                src_ref=source,
                dst_ref=target,
                send_sem=send_sem.at[way, step],
                recv_sem=recv_sem.at[way, step],
                device_id={"fsdp": targets[way]},
                device_id_type=MESH,
            )
            copy.start()
            copies[way].append(copy)
    for way in (0, 1):
        copies[way][count - 2].wait_recv()
        for copy in copies[way]:
            copy.wait_send()
    local.wait()


def ring_gather(shard):
    count = lax.axis_size("fsdp")
    rows, width = shard.shape
    split = (width // LANES + 1) // 2 * LANES
    return pl.pallas_call(
        partial(gather_kernel, count, split),
        out_shape=jax.ShapeDtypeStruct((count, rows, width), shard.dtype),
        in_specs=[VMEM_SPEC],
        out_specs=pl.BlockSpec(memory_space=pl.ANY),
        scratch_shapes=[
            pltpu.SemaphoreType.DMA,
            pltpu.SemaphoreType.DMA((2, count - 1)),
            pltpu.SemaphoreType.DMA((2, count - 1)),
        ],
        compiler_params=pltpu.CompilerParams(collective_id=0, has_side_effects=True),
        name="ring_gather",
    )(shard).reshape(count * rows, width)


def scatter_kernel(count, split, g_ref, o_ref, up_ref, down_ref, send_sem, recv_sem):
    me, position, targets = ring_setup(count)
    width = g_ref.shape[2]
    columns = (pl.ds(0, split), pl.ds(split, width - split))
    slots = (up_ref, down_ref)
    copies = [[], []]
    for step in range(count - 1):
        for way in (0, 1):
            shift = 2 * count - 1 - step if way == 0 else 1 + step
            block = ring_index((position + shift) % count, count)
            if step == 0:
                source = g_ref.at[block, :, columns[way]]
            else:
                copies[way][step - 1].wait_recv()
                held = slots[way]
                held[step - 1] = (
                    held[step - 1].astype(jnp.float32)
                    + g_ref[block, :, columns[way]].astype(jnp.float32)
                ).astype(held.dtype)
                source = held.at[step - 1]
            copy = pltpu.make_async_remote_copy(
                src_ref=source,
                dst_ref=slots[way].at[step],
                send_sem=send_sem.at[way, step],
                recv_sem=recv_sem.at[way, step],
                device_id={"fsdp": targets[way]},
                device_id_type=MESH,
            )
            copy.start()
            copies[way].append(copy)
    for way in (0, 1):
        copies[way][count - 2].wait_recv()
        o_ref[:, columns[way]] = slots[way][count - 2].astype(jnp.float32) + g_ref[
            me, :, columns[way]
        ].astype(jnp.float32)
        for copy in copies[way]:
            copy.wait_send()


def ring_scatter(blocks):
    count, rows, width = blocks.shape
    split = (width // LANES + 1) // 2 * LANES
    return pl.pallas_call(
        partial(scatter_kernel, count, split),
        out_shape=jax.ShapeDtypeStruct((rows, width), jnp.float32),
        in_specs=[VMEM_SPEC],
        out_specs=VMEM_SPEC,
        scratch_shapes=[
            pltpu.VMEM((count - 1, rows, split), blocks.dtype),
            pltpu.VMEM((count - 1, rows, width - split), blocks.dtype),
            pltpu.SemaphoreType.DMA((2, count - 1)),
            pltpu.SemaphoreType.DMA((2, count - 1)),
        ],
        compiler_params=pltpu.CompilerParams(collective_id=1, has_side_effects=True),
        name="ring_scatter",
    )(blocks)


def group_peers(heads, tensors):
    head, tensor = lax.axis_index("head"), lax.axis_index("tensor")
    peers = []
    for offset in range(1, heads * tensors):
        peer_head = (head + offset // tensors) % heads
        peer_tensor = (tensor + offset % tensors) % tensors
        peers.append((peer_head, peer_tensor))
    return head * tensors + tensor, peers


def group_barrier(peers):
    barrier = pltpu.get_barrier_semaphore()
    for head, tensor in peers:
        pl.semaphore_signal(
            barrier, inc=1, device_id={"head": head, "tensor": tensor}, device_id_type=MESH
        )
    pl.semaphore_wait(barrier, len(peers))


def group_exchange(peers, source_of, target, send_sem, recv_sem):
    copies = []
    for place, (head, tensor) in enumerate(peers):
        copy = pltpu.make_async_remote_copy(
            src_ref=source_of(head, tensor),
            dst_ref=target,
            send_sem=send_sem.at[place],
            recv_sem=recv_sem.at[place],
            device_id={"head": head, "tensor": tensor},
            device_id_type=MESH,
        )
        copy.start()
        copies.append(copy)
    return copies


def group_sum_kernel(heads, tensors, scattered, x_ref, o_ref, held, send_sem, recv_sem):
    me, peers = group_peers(heads, tensors)
    group_barrier(peers)

    def source_of(head, tensor):
        return x_ref.at[head * tensors + tensor] if scattered else x_ref

    copies = group_exchange(peers, source_of, held.at[me], send_sem, recv_sem)
    held[me] = x_ref[me] if scattered else x_ref[...]
    for copy in copies:
        copy.wait_recv()
    total = held[0].astype(jnp.float32)
    for place in range(1, heads * tensors):
        total = total + held[place].astype(jnp.float32)
    o_ref[...] = total
    for copy in copies:
        copy.wait_send()


def group_sum(x, scattered, collective):
    heads, tensors = lax.axis_size("head"), lax.axis_size("tensor")
    size = heads * tensors
    shape = x.shape[1:] if scattered else x.shape
    return pl.pallas_call(
        partial(group_sum_kernel, heads, tensors, scattered),
        out_shape=jax.ShapeDtypeStruct(shape, jnp.float32),
        in_specs=[VMEM_SPEC],
        out_specs=VMEM_SPEC,
        scratch_shapes=[
            pltpu.VMEM((size,) + shape, x.dtype),
            pltpu.SemaphoreType.DMA((size - 1,)),
            pltpu.SemaphoreType.DMA((size - 1,)),
        ],
        compiler_params=pltpu.CompilerParams(collective_id=collective, has_side_effects=True),
        name=f"group_sum_{collective}",
    )(x)


def group_gather_kernel(heads, tensors, x_ref, o_ref, send_sem, recv_sem):
    me, peers = group_peers(heads, tensors)
    group_barrier(peers)
    copies = group_exchange(peers, lambda head, tensor: x_ref, o_ref.at[me], send_sem, recv_sem)
    o_ref[me] = x_ref[...]
    for copy in copies:
        copy.wait_recv()
    for copy in copies:
        copy.wait_send()


def group_gather(x, collective):
    heads, tensors = lax.axis_size("head"), lax.axis_size("tensor")
    size = heads * tensors
    return pl.pallas_call(
        partial(group_gather_kernel, heads, tensors),
        out_shape=jax.ShapeDtypeStruct((size,) + x.shape, x.dtype),
        in_specs=[VMEM_SPEC],
        out_specs=VMEM_SPEC,
        scratch_shapes=[
            pltpu.SemaphoreType.DMA((size - 1,)),
            pltpu.SemaphoreType.DMA((size - 1,)),
        ],
        compiler_params=pltpu.CompilerParams(collective_id=collective, has_side_effects=True),
        name=f"group_gather_{collective}",
    )(x)


def decay_tile(cums_col, cums_row, first_row, rows, columns):
    gap = cums_col - cums_row
    row = first_row + lax.broadcasted_iota(jnp.int32, (rows, columns), 0)
    column = lax.broadcasted_iota(jnp.int32, (rows, columns), 1)
    return jnp.exp(jnp.where(row >= column, gap, -1e30))


def last_axes(a, b):
    return lax.dot_general(a, b, (((1,), (1,)), ((), ())), preferred_element_type=jnp.float32)


def first_axes(a, b):
    return lax.dot_general(a, b, (((0,), (0,)), ((), ())), preferred_element_type=jnp.float32)


def mix_kernel(per, width, b_ref, c_ref, x_ref, step_ref, col_ref, row_ref, y_ref, scores):
    length = x_ref.shape[0]
    chunk = min(CHUNK, length)

    @pl.when(pl.program_id(0) == 0)
    def _():
        scores[...] = last_axes(c_ref[...], b_ref[...])

    for head in range(per):
        part = slice(head * width, (head + 1) * width)
        step = step_ref[0, :, head : head + 1]
        v = (x_ref[:, part].astype(jnp.float32) * step).astype(jnp.bfloat16)
        for first in range(0, length, chunk):
            seen = first + chunk
            decay = decay_tile(
                col_ref[0, first:seen, head : head + 1],
                row_ref[0, head : head + 1, :seen],
                first,
                chunk,
                seen,
            )
            a = (scores[first:seen, :seen] * decay).astype(jnp.bfloat16)
            y_ref[first:seen, part] = jnp.dot(a, v[:seen], preferred_element_type=jnp.float32)


def back_kernel(
    per, width, b_ref, c_ref, x_ref, dy_ref, y_ref, skip_ref, step_ref, col_ref, row_ref,
    dx_ref, dstep_ref, dcums_ref, db_ref, dc_ref, scores, d_scores, carried,
):
    length = x_ref.shape[0]
    chunk = min(CHUNK, length)

    @pl.when(pl.program_id(0) == 0)
    def _():
        scores[...] = last_axes(c_ref[...], b_ref[...])
        d_scores[...] = jnp.zeros_like(d_scores)

    for head in range(per):
        part = slice(head * width, (head + 1) * width)
        step = step_ref[0, :, head : head + 1]
        x = x_ref[:, part].astype(jnp.float32)
        v = (x * step).astype(jnp.bfloat16)
        dy = dy_ref[:, part]
        dy_low = dy.astype(jnp.bfloat16)
        carried[...] = jnp.zeros_like(carried)
        for first in range(0, length, chunk):
            seen = first + chunk
            decay = decay_tile(
                col_ref[0, first:seen, head : head + 1],
                row_ref[0, head : head + 1, :seen],
                first,
                chunk,
                seen,
            )
            a = (scores[first:seen, :seen] * decay).astype(jnp.bfloat16)
            carried[:seen] += first_axes(a, dy_low[first:seen])
            d_scores[first:seen, :seen] += last_axes(dy_low[first:seen], v[:seen]) * decay
        u = carried[...]
        dx_ref[:, part] = step * u + skip_ref[:, part] * dy
        dstep_ref[0, :, head : head + 1] = jnp.sum(x * u, axis=1, keepdims=True)
        dcums_ref[0, :, head : head + 1] = jnp.sum(
            dy_low.astype(jnp.float32) * y_ref[:, part] - v.astype(jnp.float32) * u,
            axis=1,
            keepdims=True,
        )

    @pl.when(pl.program_id(0) == pl.num_programs(0) - 1)
    def _():
        low = d_scores[...].astype(jnp.bfloat16)
        dc_ref[...] = jnp.dot(low, b_ref[...], preferred_element_type=jnp.float32)
        db_ref[...] = first_axes(low, c_ref[...])


def whole(shape):
    return pl.BlockSpec(shape, lambda i: (0,) * len(shape))


def head_specs(length, per, width, state):
    wide = pl.BlockSpec((length, per * width), lambda i: (0, i))
    col = pl.BlockSpec((1, length, per), lambda i: (i, 0, 0))
    row = pl.BlockSpec((1, per, length), lambda i: (i, 0, 0))
    return whole((length, state)), wide, col, row


def mix(b, c, x, step, col, row, width):
    length, inner = x.shape
    per = col.shape[2]
    maps, wide, col_spec, row_spec = head_specs(length, per, width, b.shape[1])
    return pl.pallas_call(
        partial(mix_kernel, per, width),
        grid=(inner // (per * width),),
        in_specs=[maps, maps, wide, col_spec, col_spec, row_spec],
        out_specs=wide,
        out_shape=jax.ShapeDtypeStruct((length, inner), jnp.float32),
        scratch_shapes=[pltpu.VMEM((length, length), jnp.float32)],
        name="mix",
    )(b, c, x, step, col, row)


def mix_back(b, c, x, dy, y, skip_row, step, col, row, width):
    length, inner = x.shape
    groups, _, per = col.shape
    state = b.shape[1]
    maps, wide, col_spec, row_spec = head_specs(length, per, width, state)
    return pl.pallas_call(
        partial(back_kernel, per, width),
        grid=(groups,),
        in_specs=[
            maps, maps, wide, wide, wide,
            pl.BlockSpec((1, per * width), lambda i: (0, i)),
            col_spec, col_spec, row_spec,
        ],
        out_specs=[wide, col_spec, col_spec, maps, maps],
        out_shape=[
            jax.ShapeDtypeStruct((length, inner), jnp.float32),
            jax.ShapeDtypeStruct((groups, length, per), jnp.float32),
            jax.ShapeDtypeStruct((groups, length, per), jnp.float32),
            jax.ShapeDtypeStruct((length, state), jnp.float32),
            jax.ShapeDtypeStruct((length, state), jnp.float32),
        ],
        scratch_shapes=[
            pltpu.VMEM((length, length), jnp.float32),
            pltpu.VMEM((length, length), jnp.float32),
            pltpu.VMEM((length, width), jnp.float32),
        ],
        name="mix_back",
    )(b, c, x, dy, y, skip_row, step, col, row)


def delayed(signal, count):
    return signal if count == 0 else jnp.pad(signal, ((count, 0), (0, 0)))[: signal.shape[0]]


def advanced(signal, count):
    return signal if count == 0 else jnp.pad(signal, ((0, count), (0, 0)))[count:]


def causal_conv(signal, kernel):
    taps = kernel.shape[1]
    return sum(delayed(signal, taps - 1 - k) * kernel[:, k] for k in range(taps))


def silu_slope(value):
    sigma = jax.nn.sigmoid(value)
    return sigma * (1.0 + value * (1.0 - sigma))


def conv_silu_back(raw, conv, kernel, upstream):
    taps = kernel.shape[1]
    d_conv = upstream * silu_slope(conv)
    d_raw = sum(advanced(d_conv, taps - 1 - k) * kernel[:, k] for k in range(taps))
    d_kernel = jnp.stack(
        [jnp.sum(delayed(raw, taps - 1 - k) * d_conv, axis=0) for k in range(taps)], axis=0
    )
    return d_raw, d_kernel


def pad_lanes(a):
    extra = -a.shape[-1] % LANES
    return a if extra == 0 else jnp.pad(a, ((0, 0),) * (a.ndim - 1) + ((0, extra),))


def on_device(
    block_in, cotangent, norm_gain, w_x, w_z, w_bc, w_dt, conv_x, conv_bc, dt_bias, a_log, skip,
    gate_gain, w_out,
):
    length, width = block_in.shape
    head_count, head_width, taps = conv_x.shape
    state = conv_bc.shape[1]
    inner = head_count * head_width
    heads, tensors, count = (lax.axis_size(a) for a in ("head", "tensor", "fsdp"))
    size = heads * tensors
    head_at = lax.axis_index("head")
    group_at = head_at * tensors + lax.axis_index("tensor")
    quarter = 2 * state // size
    rows = w_x.shape[0]
    owned = length // size
    full_inner = inner * size

    packed = jnp.concatenate(
        [
            w_x.reshape(rows, inner),
            w_z.reshape(rows, inner),
            w_bc.reshape(rows, 2 * state),
            pad_lanes(w_dt),
            w_out.reshape(inner, rows).T,
        ],
        axis=1,
    )
    weights = ring_gather(packed)
    dt_at = 2 * inner + 2 * state
    out_at = packed.shape[1] - inner
    weight_out = weights[:, out_at:]
    features = block_in.astype(jnp.float32)
    scale_in = lax.rsqrt(jnp.mean(features * features, axis=1, keepdims=True) + EPSILON)
    normed = (features * scale_in * norm_gain).astype(jnp.bfloat16)
    raw = jnp.dot(normed, weights[:, :out_at], preferred_element_type=jnp.float32)
    x_raw = raw[:, :inner]
    z_raw = raw[:, inner : 2 * inner]
    bc_raw = raw[:, 2 * inner : dt_at]
    dt_in = raw[:, dt_at : dt_at + head_count] + dt_bias
    kernel_x = conv_x.reshape(inner, taps)
    kernel_bc = conv_bc.reshape(2 * state, taps)
    gain = gate_gain.reshape(inner)
    x_conv = causal_conv(x_raw, kernel_x)
    x_act = jax.nn.silu(x_conv).astype(jnp.bfloat16)
    bc_act = jax.nn.silu(causal_conv(bc_raw, kernel_bc)).astype(jnp.bfloat16)
    b_maps, c_maps = bc_act[:, :state], bc_act[:, state:]

    per = max(1, LANES // head_width)
    step = jax.nn.softplus(dt_in)
    rate = -jnp.exp(a_log)
    at = jnp.arange(length)
    lower = (at[:, None] >= at[None, :]).astype(jnp.float32)
    cums = jnp.dot(lower, step * rate, precision=PRECISE)

    def as_columns(a):
        return a.reshape(length, head_count // per, per).transpose(1, 0, 2)

    def from_columns(a):
        return a.transpose(1, 0, 2).reshape(length, head_count)

    step_col = as_columns(step)
    col = as_columns(cums)
    row = cums.T.reshape(head_count // per, per, length)
    scanned = mix(b_maps, c_maps, x_act, step_col, col, row, head_width)
    skip_row = jnp.repeat(skip, head_width)[None, :]
    x_wide = x_act.astype(jnp.float32)
    mixed = scanned + skip_row * x_wide
    z_sigma = jax.nn.sigmoid(z_raw)
    z_silu = z_raw * z_sigma
    gated = mixed * z_silu
    d_normed_out = jnp.dot(cotangent, weight_out, preferred_element_type=jnp.float32)
    d_hat = d_normed_out * gain
    sums = jnp.concatenate([jnp.sum(gated * gated, axis=1), jnp.sum(d_hat * gated, axis=1)])
    sums = group_sum(sums.reshape(-1, LANES), False, 2).reshape(2, length)
    scale_out = lax.rsqrt(sums[0] / full_inner + EPSILON)[:, None]
    inner_sum = sums[1][:, None]
    normed_out = (gated * scale_out * gain).astype(jnp.bfloat16)
    partial_out = last_axes(normed_out, weight_out).astype(jnp.bfloat16)
    mine = lambda a: lax.dynamic_slice_in_dim(a, group_at * owned, owned, 0)
    summed = group_sum(partial_out.reshape(size, owned, width), True, 3)
    own_out = (summed + mine(features)).astype(jnp.bfloat16)
    block_out = group_gather(own_out, 4).reshape(length, width)

    g_gate_gain = jnp.sum(d_normed_out * gated * scale_out, axis=0)
    d_gated = scale_out * d_hat - gated * scale_out**3 * (inner_sum / full_inner)
    d_mixed = d_gated * z_silu
    d_z = (d_gated * mixed * (z_sigma * (1.0 + z_raw * (1.0 - z_sigma)))).astype(jnp.bfloat16)
    d_xs, d_step, d_cums, d_b, d_c = mix_back(
        b_maps, c_maps, x_act, d_mixed, scanned, skip_row, step_col, col, row, head_width
    )
    d_logs = jnp.dot(lower.T, from_columns(d_cums), precision=PRECISE)
    d_step = from_columns(d_step) + d_logs * rate
    d_dt_part = d_step * jax.nn.sigmoid(dt_in)
    g_a_log = jnp.sum(d_logs * step, axis=0) * rate
    g_skip = jnp.sum((d_mixed * x_wide).reshape(length, head_count, head_width), axis=(0, 2))

    d_bc_part = jnp.concatenate([d_b, d_c], axis=1)
    pieces = []
    for place in range(size):
        same = (head_at == place // tensors).astype(jnp.float32)
        pieces.append(
            pad_lanes(
                jnp.concatenate(
                    [d_bc_part[:, place * quarter : (place + 1) * quarter], d_dt_part * same], axis=1
                )
            )
        )
    d_small = group_sum(jnp.stack(pieces).astype(jnp.bfloat16), True, 5)
    d_bc = d_small[:, :quarter]
    d_dt = d_small[:, quarter : quarter + head_count]
    g_dt_bias = jnp.sum(d_dt, axis=0)

    own_cols = lambda a, axis: lax.dynamic_slice_in_dim(a, group_at * quarter, quarter, axis)
    bc_raw_own = own_cols(bc_raw, 1)
    kernel_bc_own = own_cols(kernel_bc, 0)
    d_bc_raw, g_conv_bc = conv_silu_back(
        bc_raw_own, causal_conv(bc_raw_own, kernel_bc_own), kernel_bc_own, d_bc
    )
    d_x_raw, g_conv_x = conv_silu_back(x_raw, x_conv, kernel_x, d_xs)
    d_cat = jnp.concatenate(
        [
            d_x_raw.astype(jnp.bfloat16),
            d_z,
            pad_lanes(jnp.concatenate([d_bc_raw, d_dt], axis=1).astype(jnp.bfloat16)),
        ],
        axis=1,
    )
    only = (lax.axis_index("tensor") == 0).astype(jnp.bfloat16)
    side = pad_lanes(
        jnp.concatenate(
            [own_cols(weights[:, 2 * inner : dt_at], 1), weights[:, dt_at : dt_at + head_count] * only],
            axis=1,
        )
    )
    local_part = last_axes(d_cat[:, : 2 * inner], weights[:, : 2 * inner]) + last_axes(
        d_cat[:, 2 * inner :], side
    )
    d_normed = group_sum(local_part.astype(jnp.bfloat16).reshape(size, owned, width), True, 6)
    own_features, own_scale = mine(features), mine(scale_in)
    g_norm_gain = jnp.sum(d_normed * own_features * own_scale, axis=0)
    d_in_hat = d_normed * norm_gain
    own_grad = own_scale * d_in_hat - own_features * own_scale**3 * jnp.mean(
        d_in_hat * own_features, axis=1, keepdims=True
    )
    others = group_gather(own_grad.astype(jnp.bfloat16), 7).reshape(length, width)
    grad_in = others.astype(jnp.float32) + cotangent.astype(jnp.float32)

    grads = jnp.concatenate(
        [
            first_axes(normed, d_cat).astype(jnp.bfloat16),
            first_axes(cotangent, normed_out).astype(jnp.bfloat16),
        ],
        axis=1,
    )
    own = ring_scatter(grads.reshape(count, rows, grads.shape[1]))
    side_at = 2 * inner
    g_w_bc = group_gather(pad_lanes(own[:, side_at : side_at + quarter]), 8)[:, :, :quarter]
    g_w_bc = g_w_bc.transpose(1, 0, 2).reshape(rows, 2, state)

    small = lax.psum(
        jnp.concatenate(
            [g_norm_gain, g_conv_x.reshape(-1), g_gate_gain, g_conv_bc.reshape(-1), g_dt_bias, g_a_log, g_skip]
        ),
        "fsdp",
    )
    cuts = []
    start = 0
    for amount in (width, taps * inner, inner, taps * quarter, head_count, head_count, head_count):
        cuts.append(small[start : start + amount])
        start += amount
    spread = jnp.zeros((2 * state, taps), jnp.float32)
    spread = lax.dynamic_update_slice_in_dim(
        spread, cuts[3].reshape(taps, quarter).T, group_at * quarter, 0
    )
    by_head = jnp.zeros((heads, 2 * head_count), jnp.float32)
    by_head = lax.dynamic_update_slice_in_dim(
        by_head, jnp.concatenate([cuts[5], cuts[6]])[None], head_at, 0
    )
    last = jnp.concatenate([cuts[0], spread.reshape(-1), by_head.reshape(-1)])
    total = last.shape[0]
    last = jnp.pad(last, (0, -total % (8 * LANES))).reshape(-1, LANES)
    last = group_sum(last, False, 9).reshape(-1)
    at_heads = width + 2 * state * taps
    mine_head = lax.dynamic_slice_in_dim(
        last[at_heads:total].reshape(heads, 2 * head_count), head_at, 1, 0
    )[0]
    return (
        block_out,
        grad_in,
        last[:width],
        own[:, :inner].reshape(rows, head_count, head_width),
        own[:, inner : 2 * inner].reshape(rows, head_count, head_width),
        g_w_bc,
        own[:, side_at + quarter : side_at + quarter + head_count],
        cuts[1].reshape(taps, inner).T.reshape(head_count, head_width, taps),
        last[width:at_heads].reshape(2, state, taps),
        cuts[4],
        mine_head[:head_count],
        mine_head[head_count:],
        cuts[2].reshape(head_count, head_width),
        own[:, own.shape[1] - inner :].T.reshape(head_count, head_width, rows),
    )


def solution(mesh):
    return jax.shard_map(
        on_device,
        mesh=mesh,
        in_specs=(
            P("fsdp", None),
            P("fsdp", None),
            P(),
            P("fsdp", "head", "tensor"),
            P("fsdp", "head", "tensor"),
            P("fsdp", None, None),
            P("fsdp", "head"),
            P("head", "tensor", None),
            P(),
            P("head"),
            P("head"),
            P("head"),
            P("head", "tensor"),
            P("head", "tensor", "fsdp"),
        ),
        out_specs=(
            P("fsdp", None),
            P("fsdp", None),
            P(),
            P("fsdp", "head", "tensor"),
            P("fsdp", "head", "tensor"),
            P("fsdp", None, None),
            P("fsdp", "head"),
            P("head", "tensor", None),
            P(),
            P("head"),
            P("head"),
            P("head"),
            P("head", "tensor"),
            P("head", "tensor", "fsdp"),
        ),
        check_vma=False,
    )
```

```python
from functools import partial

import jax
import jax.numpy as jnp
from jax import lax
from jax.experimental import pallas as pl
from jax.experimental.pallas import tpu as pltpu
from jax.sharding import PartitionSpec as P

EPSILON = 1e-05
PRECISE = lax.Precision.HIGHEST
LANES = 128
CHUNK = 256
WAYS = 4
MESH = pl.DeviceIdType.MESH
VMEM_SPEC = pl.BlockSpec(memory_space=pltpu.VMEM)


def ring_index(position, count):
    high = position // (count // 2)
    return (1 - high) * 2 * position + high * (2 * (count - 1 - position) + 1)


def ring_position(index, count):
    odd = index % 2
    return (1 - odd) * (index // 2) + odd * (count - 1 - index // 2)


def ring_setup(count):
    me = lax.axis_index("fsdp")
    position = ring_position(me, count)
    right = ring_index((position + 1) % count, count)
    left = ring_index((position + count - 1) % count, count)
    barrier = pltpu.get_barrier_semaphore()
    for neighbour in (left, right):
        pl.semaphore_signal(barrier, inc=1, device_id={"fsdp": neighbour}, device_id_type=MESH)
    pl.semaphore_wait(barrier, 2)
    return me, position, (right, left)


def column_ways(width):
    tiles = width // LANES
    share, extra = tiles // WAYS, tiles % WAYS
    cuts, start = [], 0
    for way in range(WAYS):
        amount = (share + (1 if way < extra else 0)) * LANES
        cuts.append((start, amount))
        start += amount
    return cuts


def gather_kernel(count, x_ref, o_ref, local_sem, send_sem, recv_sem):
    me, position, targets = ring_setup(count)
    local = pltpu.make_async_copy(x_ref, o_ref.at[me], local_sem)
    local.start()
    ways = column_ways(x_ref.shape[1])
    copies = [[] for _ in ways]
    for step in range(count - 1):
        for way, (start, amount) in enumerate(ways):
            shift = count - step if way % 2 == 0 else step
            block = ring_index((position + shift) % count, count)
            columns = pl.ds(start, amount)
            target = o_ref.at[block, :, columns]
            source = x_ref.at[:, columns] if step == 0 else target
            if step > 0:
                copies[way][step - 1].wait_recv()
            copy = pltpu.make_async_remote_copy(
                src_ref=source,
                dst_ref=target,
                send_sem=send_sem.at[way, step],
                recv_sem=recv_sem.at[way, step],
                device_id={"fsdp": targets[way % 2]},
                device_id_type=MESH,
            )
            copy.start()
            copies[way].append(copy)
    for way in range(len(ways)):
        copies[way][count - 2].wait_recv()
        for copy in copies[way]:
            copy.wait_send()
    local.wait()


def ring_gather(shard):
    count = lax.axis_size("fsdp")
    rows, width = shard.shape
    return pl.pallas_call(
        partial(gather_kernel, count),
        out_shape=jax.ShapeDtypeStruct((count, rows, width), shard.dtype),
        in_specs=[VMEM_SPEC],
        out_specs=pl.BlockSpec(memory_space=pl.ANY),
        scratch_shapes=[
            pltpu.SemaphoreType.DMA,
            pltpu.SemaphoreType.DMA((WAYS, count - 1)),
            pltpu.SemaphoreType.DMA((WAYS, count - 1)),
        ],
        compiler_params=pltpu.CompilerParams(collective_id=0, has_side_effects=True),
        name="ring_gather",
    )(shard).reshape(count * rows, width)


def send(source, target, sems, place, device):
    copy = pltpu.make_async_remote_copy(
        src_ref=source,
        dst_ref=target,
        send_sem=sems[0].at[place],
        recv_sem=sems[1].at[place],
        device_id=device,
        device_id_type=MESH,
    )
    copy.start()
    return copy


def closing_kernel(
    count, heads, tensors, side_at,
    g_ref, dn_ref, po_ref, feat_ref, scale_ref, gain_ref, lone_ref, shared_ref,
    own_ref, out_ref, grad_ref, bc_ref, lone_out, shared_out, norm_out,
    *scratch,
):
    slots = scratch[:WAYS]
    (held_a, stage, held_b, norm_own, norm_held, norm_sum, shared_held, shared_sum,
     lone_all, shared_all, norm_all) = scratch[WAYS : WAYS + 11]
    sem = scratch[WAYS + 11 :]
    pairs = [(sem[2 * i], sem[2 * i + 1]) for i in range(len(sem) // 2)]
    ring_sems, a_sems, b_sems, at_sems, ah_sems, group_sems, lone_sems, late_sems, bc_sems = pairs
    me = lax.axis_index("fsdp")
    position = ring_position(me, count)
    targets = (
        ring_index((position + 1) % count, count),
        ring_index((position + count - 1) % count, count),
    )
    group_me, peers = group_peers(heads, tensors)
    head, tensor = lax.axis_index("head"), lax.axis_index("tensor")
    others = [(me + offset) % count for offset in range(1, count)]
    barrier = pltpu.get_barrier_semaphore()
    for h, t in peers:
        pl.semaphore_signal(barrier, inc=1, device_id={"head": h, "tensor": t}, device_id_type=MESH)
    for other in others:
        pl.semaphore_signal(barrier, inc=1, device_id={"fsdp": other}, device_id_type=MESH)
    pl.semaphore_wait(barrier, len(peers) + len(others))

    started = []

    def sent(*args):
        copy = send(*args)
        started.append(copy)
        return copy

    head_peers = [(head + offset) % heads for offset in range(1, heads)]
    tensor_peers = [(tensor + offset) % tensors for offset in range(1, tensors)]
    parts = (dn_ref, po_ref)
    results = (grad_ref, out_ref)
    phase = {}

    def start_a():
        for i, ref in enumerate(parts):
            phase["a", i] = [
                sent(
                    ref.at[pl.ds(peer * tensors, tensors)], held_a.at[i, k], a_sems, (i, k),
                    {"head": peer},
                )
                for k, peer in enumerate(head_peers)
            ]
        phase["lone"] = [
            sent(lone_ref, lone_all.at[me], lone_sems, k, {"fsdp": other})
            for k, other in enumerate(others)
        ]
        lone_all[me] = lone_ref[...]

    def to_b(i):
        for copy in phase["a", i]:
            copy.wait_recv()
        for t in range(tensors):
            total = parts[i][head * tensors + t].astype(jnp.float32)
            for k in range(heads - 1):
                total = total + held_a[i, k, t].astype(jnp.float32)
            stage[i, t] = total.astype(stage.dtype)
        phase["b", i] = [
            sent(stage.at[i, peer], held_b.at[i, k], b_sems, (i, k), {"tensor": peer})
            for k, peer in enumerate(tensor_peers)
        ]

    def spread(i):
        for copy in phase["b", i]:
            copy.wait_recv()
        total = stage[i, tensor].astype(jnp.float32)
        for k in range(tensors - 1):
            total = total + held_b[i, k].astype(jnp.float32)
        features = feat_ref[...]
        if i == 0:
            scale = scale_ref[...]
            norm_own[...] = jnp.sum(total * (features * scale), axis=0, keepdims=True)
            inner = total * gain_ref[...]
            mean = jnp.mean(inner * features, axis=1, keepdims=True)
            value = scale * inner - features * (scale * scale * scale * mean)
        else:
            value = total + features
        result = results[i]
        result[group_me] = value.astype(result.dtype)
        mine = result.at[group_me]
        phase["t", i] = [
            sent(mine, mine, at_sems, (i, k), {"tensor": peer}) for k, peer in enumerate(tensor_peers)
        ]
        phase["h", i] = [
            sent(mine, mine, ah_sems, (i, k, 0), {"head": peer}) for k, peer in enumerate(head_peers)
        ]
        if i == 0:
            norm_held[group_me] = norm_own[...]
            shared_held[group_me] = shared_ref[...]
            phase["group"] = []
            for k, (h, t) in enumerate(peers):
                device = {"head": h, "tensor": t}
                phase["group"] += [
                    sent(norm_own, norm_held.at[group_me], group_sems, (0, k), device),
                    sent(shared_ref, shared_held.at[group_me], group_sems, (1, k), device),
                ]

    def forward(i):
        result = results[i]
        for k, copy in enumerate(phase["t", i]):
            copy.wait_recv()
            block = result.at[head * tensors + (tensor + tensors - 1 - k) % tensors]
            phase["h", i] += [
                sent(block, block, ah_sems, (i, j, k + 1), {"head": peer})
                for j, peer in enumerate(head_peers)
            ]

    def late():
        for copy in phase["group"]:
            copy.wait_recv()
        for held, total, everyone, place in (
            (norm_held, norm_sum, norm_all, 0),
            (shared_held, shared_sum, shared_all, 1),
        ):
            value = held[0]
            for k in range(1, heads * tensors):
                value = value + held[k]
            total[...] = value
            everyone[me] = value
            phase["late", place] = [
                sent(total, everyone.at[me], late_sems, (place, k), {"fsdp": other})
                for k, other in enumerate(others)
            ]

    events = [
        (0, start_a),
        (1, lambda: to_b(0)), (1, lambda: to_b(1)),
        (2, lambda: spread(0)), (3, lambda: spread(1)),
        (4, lambda: forward(0)), (4, late), (5, lambda: forward(1)),
    ]
    ways = column_ways(g_ref.shape[2])
    ring = [[] for _ in ways]
    for step in range(count - 1):
        for way, (start, amount) in enumerate(ways):
            columns = pl.ds(start, amount)
            shift = 2 * count - 1 - step if way % 2 == 0 else 1 + step
            block = ring_index((position + shift) % count, count)
            held = slots[way]
            if step == 0:
                source = g_ref.at[block, :, columns]
            else:
                ring[way][step - 1].wait_recv()
                held[step - 1] = (
                    held[step - 1].astype(jnp.float32)
                    + g_ref[block, :, columns].astype(jnp.float32)
                ).astype(held.dtype)
                source = held.at[step - 1]
            ring[way].append(
                sent(source, held.at[step], ring_sems, (way, step), {"fsdp": targets[way % 2]})
            )
        while events and events[0][0] <= step:
            events.pop(0)[1]()
    for _, event in events:
        event()
    side = pl.ds(side_at, LANES)
    order = sorted(
        range(len(ways)), key=lambda way: not ways[way][0] <= side_at < ways[way][0] + ways[way][1]
    )
    for way in order:
        start, amount = ways[way]
        columns = pl.ds(start, amount)
        ring[way][count - 2].wait_recv()
        own_ref[:, columns] = slots[way][count - 2].astype(jnp.float32) + g_ref[
            me, :, columns
        ].astype(jnp.float32)
        if start <= side_at < start + amount:
            bc_ref[group_me] = own_ref[:, side]
            bc_copies = [
                sent(bc_ref.at[group_me], bc_ref.at[group_me], bc_sems, k, {"head": h, "tensor": t})
                for k, (h, t) in enumerate(peers)
            ]
    for copies, everyone, total in (
        (phase["lone"], lone_all, lone_out),
        (phase["late", 0], norm_all, norm_out),
        (phase["late", 1], shared_all, shared_out),
    ):
        for copy in copies:
            copy.wait_recv()
        value = everyone[0]
        for k in range(1, count):
            value = value + everyone[k]
        total[...] = value
    for i in range(2):
        for copy in phase["h", i]:
            copy.wait_recv()
    for copy in bc_copies:
        copy.wait_recv()
    for copy in started:
        copy.wait_send()


def closing(grads, d_normed, partial_out, features, scale, gain, lone, shared, side_at):
    count, heads, tensors = (lax.axis_size(a) for a in ("fsdp", "head", "tensor"))
    size = heads * tensors
    _, rows, columns = grads.shape
    _, owned, width = d_normed.shape
    low, full = grads.dtype, jnp.float32
    ways = column_ways(columns)
    assert all(amount > 0 for _, amount in ways)
    dma = pltpu.SemaphoreType.DMA
    shapes = [
        (WAYS, count - 1), (2, heads - 1), (2, tensors - 1), (2, tensors - 1),
        (2, heads - 1, tensors), (2, size - 1), (count - 1,), (2, count - 1), (size - 1,),
    ]
    return pl.pallas_call(
        partial(closing_kernel, count, heads, tensors, side_at),
        out_shape=[
            jax.ShapeDtypeStruct((rows, columns), full),
            jax.ShapeDtypeStruct((size, owned, width), low),
            jax.ShapeDtypeStruct((size, owned, width), low),
            jax.ShapeDtypeStruct((size, rows, LANES), full),
            jax.ShapeDtypeStruct(lone.shape, full),
            jax.ShapeDtypeStruct(shared.shape, full),
            jax.ShapeDtypeStruct((1, width), full),
        ],
        in_specs=[VMEM_SPEC] * 8,
        out_specs=[VMEM_SPEC] * 7,
        scratch_shapes=[pltpu.VMEM((count - 1, rows, amount), low) for _, amount in ways]
        + [
            pltpu.VMEM((2, heads - 1, tensors, owned, width), low),
            pltpu.VMEM((2, tensors, owned, width), low),
            pltpu.VMEM((2, tensors - 1, owned, width), low),
            pltpu.VMEM((1, width), full),
            pltpu.VMEM((size, 1, width), full),
            pltpu.VMEM((1, width), full),
            pltpu.VMEM((size,) + shared.shape, full),
            pltpu.VMEM(shared.shape, full),
            pltpu.VMEM((count,) + lone.shape, full),
            pltpu.VMEM((count,) + shared.shape, full),
            pltpu.VMEM((count, 1, width), full),
        ]
        + [dma(shape) for shape in shapes for _ in range(2)],
        compiler_params=pltpu.CompilerParams(collective_id=1, has_side_effects=True),
        name="closing",
    )(grads, d_normed, partial_out, features, scale, gain, lone, shared)


def group_peers(heads, tensors):
    head, tensor = lax.axis_index("head"), lax.axis_index("tensor")
    peers = []
    for offset in range(1, heads * tensors):
        peer_head = (head + offset // tensors) % heads
        peer_tensor = (tensor + offset % tensors) % tensors
        peers.append((peer_head, peer_tensor))
    return head * tensors + tensor, peers


def group_barrier(peers):
    barrier = pltpu.get_barrier_semaphore()
    for head, tensor in peers:
        pl.semaphore_signal(
            barrier, inc=1, device_id={"head": head, "tensor": tensor}, device_id_type=MESH
        )
    pl.semaphore_wait(barrier, len(peers))


def group_exchange(peers, source_of, target, send_sem, recv_sem):
    copies = []
    for place, (head, tensor) in enumerate(peers):
        copy = pltpu.make_async_remote_copy(
            src_ref=source_of(head, tensor),
            dst_ref=target,
            send_sem=send_sem.at[place],
            recv_sem=recv_sem.at[place],
            device_id={"head": head, "tensor": tensor},
            device_id_type=MESH,
        )
        copy.start()
        copies.append(copy)
    return copies


def group_sum_kernel(heads, tensors, scattered, x_ref, o_ref, held, send_sem, recv_sem):
    me, peers = group_peers(heads, tensors)
    group_barrier(peers)

    def source_of(head, tensor):
        return x_ref.at[head * tensors + tensor] if scattered else x_ref

    copies = group_exchange(peers, source_of, held.at[me], send_sem, recv_sem)
    held[me] = x_ref[me] if scattered else x_ref[...]
    for copy in copies:
        copy.wait_recv()
    total = held[0].astype(jnp.float32)
    for place in range(1, heads * tensors):
        total = total + held[place].astype(jnp.float32)
    o_ref[...] = total
    for copy in copies:
        copy.wait_send()


def group_sum(x, scattered, collective):
    heads, tensors = lax.axis_size("head"), lax.axis_size("tensor")
    size = heads * tensors
    shape = x.shape[1:] if scattered else x.shape
    return pl.pallas_call(
        partial(group_sum_kernel, heads, tensors, scattered),
        out_shape=jax.ShapeDtypeStruct(shape, jnp.float32),
        in_specs=[VMEM_SPEC],
        out_specs=VMEM_SPEC,
        scratch_shapes=[
            pltpu.VMEM((size,) + shape, x.dtype),
            pltpu.SemaphoreType.DMA((size - 1,)),
            pltpu.SemaphoreType.DMA((size - 1,)),
        ],
        compiler_params=pltpu.CompilerParams(collective_id=collective, has_side_effects=True),
        name=f"group_sum_{collective}",
    )(x)


def decay_tile(cums_col, cums_row, first_row, rows, columns):
    gap = cums_col - cums_row
    row = first_row + lax.broadcasted_iota(jnp.int32, (rows, columns), 0)
    column = lax.broadcasted_iota(jnp.int32, (rows, columns), 1)
    return jnp.exp(jnp.where(row >= column, gap, -1e30))


def last_axes(a, b):
    return lax.dot_general(a, b, (((1,), (1,)), ((), ())), preferred_element_type=jnp.float32)


def first_axes(a, b):
    return lax.dot_general(a, b, (((0,), (0,)), ((), ())), preferred_element_type=jnp.float32)


def mix_kernel(per, width, b_ref, c_ref, x_ref, step_ref, col_ref, row_ref, y_ref, scores):
    length = x_ref.shape[0]
    chunk = min(CHUNK, length)

    @pl.when(pl.program_id(0) == 0)
    def _():
        scores[...] = last_axes(c_ref[...], b_ref[...])

    for head in range(per):
        part = slice(head * width, (head + 1) * width)
        step = step_ref[0, :, head : head + 1]
        v = (x_ref[:, part].astype(jnp.float32) * step).astype(jnp.bfloat16)
        for first in range(0, length, chunk):
            seen = first + chunk
            decay = decay_tile(
                col_ref[0, first:seen, head : head + 1],
                row_ref[0, head : head + 1, :seen],
                first,
                chunk,
                seen,
            )
            a = (scores[first:seen, :seen] * decay).astype(jnp.bfloat16)
            y_ref[first:seen, part] = jnp.dot(a, v[:seen], preferred_element_type=jnp.float32)


def back_kernel(
    per, width, b_ref, c_ref, x_ref, dy_ref, y_ref, skip_ref, step_ref, col_ref, row_ref,
    dx_ref, dstep_ref, dcums_ref, db_ref, dc_ref, scores, d_scores, carried,
):
    length = x_ref.shape[0]
    chunk = min(CHUNK, length)

    @pl.when(pl.program_id(0) == 0)
    def _():
        scores[...] = last_axes(c_ref[...], b_ref[...])
        d_scores[...] = jnp.zeros_like(d_scores)

    for head in range(per):
        part = slice(head * width, (head + 1) * width)
        step = step_ref[0, :, head : head + 1]
        x = x_ref[:, part].astype(jnp.float32)
        v = (x * step).astype(jnp.bfloat16)
        dy = dy_ref[:, part]
        dy_low = dy.astype(jnp.bfloat16)
        carried[...] = jnp.zeros_like(carried)
        for first in range(0, length, chunk):
            seen = first + chunk
            decay = decay_tile(
                col_ref[0, first:seen, head : head + 1],
                row_ref[0, head : head + 1, :seen],
                first,
                chunk,
                seen,
            )
            a = (scores[first:seen, :seen] * decay).astype(jnp.bfloat16)
            carried[:seen] += first_axes(a, dy_low[first:seen])
            d_scores[first:seen, :seen] += last_axes(dy_low[first:seen], v[:seen]) * decay
        u = carried[...]
        dx_ref[:, part] = step * u + skip_ref[:, part] * dy
        dstep_ref[0, :, head : head + 1] = jnp.sum(x * u, axis=1, keepdims=True)
        dcums_ref[0, :, head : head + 1] = jnp.sum(
            dy_low.astype(jnp.float32) * y_ref[:, part] - v.astype(jnp.float32) * u,
            axis=1,
            keepdims=True,
        )

    @pl.when(pl.program_id(0) == pl.num_programs(0) - 1)
    def _():
        low = d_scores[...].astype(jnp.bfloat16)
        dc_ref[...] = jnp.dot(low, b_ref[...], preferred_element_type=jnp.float32)
        db_ref[...] = first_axes(low, c_ref[...])


def whole(shape):
    return pl.BlockSpec(shape, lambda i: (0,) * len(shape))


def head_specs(length, per, width, state):
    wide = pl.BlockSpec((length, per * width), lambda i: (0, i))
    col = pl.BlockSpec((1, length, per), lambda i: (i, 0, 0))
    row = pl.BlockSpec((1, per, length), lambda i: (i, 0, 0))
    return whole((length, state)), wide, col, row


def mix(b, c, x, step, col, row, width):
    length, inner = x.shape
    per = col.shape[2]
    maps, wide, col_spec, row_spec = head_specs(length, per, width, b.shape[1])
    return pl.pallas_call(
        partial(mix_kernel, per, width),
        grid=(inner // (per * width),),
        in_specs=[maps, maps, wide, col_spec, col_spec, row_spec],
        out_specs=wide,
        out_shape=jax.ShapeDtypeStruct((length, inner), jnp.float32),
        scratch_shapes=[pltpu.VMEM((length, length), jnp.float32)],
        name="mix",
    )(b, c, x, step, col, row)


def mix_back(b, c, x, dy, y, skip_row, step, col, row, width):
    length, inner = x.shape
    groups, _, per = col.shape
    state = b.shape[1]
    maps, wide, col_spec, row_spec = head_specs(length, per, width, state)
    return pl.pallas_call(
        partial(back_kernel, per, width),
        grid=(groups,),
        in_specs=[
            maps, maps, wide, wide, wide,
            pl.BlockSpec((1, per * width), lambda i: (0, i)),
            col_spec, col_spec, row_spec,
        ],
        out_specs=[wide, col_spec, col_spec, maps, maps],
        out_shape=[
            jax.ShapeDtypeStruct((length, inner), jnp.float32),
            jax.ShapeDtypeStruct((groups, length, per), jnp.float32),
            jax.ShapeDtypeStruct((groups, length, per), jnp.float32),
            jax.ShapeDtypeStruct((length, state), jnp.float32),
            jax.ShapeDtypeStruct((length, state), jnp.float32),
        ],
        scratch_shapes=[
            pltpu.VMEM((length, length), jnp.float32),
            pltpu.VMEM((length, length), jnp.float32),
            pltpu.VMEM((length, width), jnp.float32),
        ],
        name="mix_back",
    )(b, c, x, dy, y, skip_row, step, col, row)


def delayed(signal, count):
    return signal if count == 0 else jnp.pad(signal, ((count, 0), (0, 0)))[: signal.shape[0]]


def advanced(signal, count):
    return signal if count == 0 else jnp.pad(signal, ((0, count), (0, 0)))[count:]


def causal_conv(signal, kernel):
    taps = kernel.shape[1]
    return sum(delayed(signal, taps - 1 - k) * kernel[:, k] for k in range(taps))


def silu_slope(value):
    sigma = jax.nn.sigmoid(value)
    return sigma * (1.0 + value * (1.0 - sigma))


def conv_silu_back(raw, conv, kernel, upstream):
    taps = kernel.shape[1]
    d_conv = upstream * silu_slope(conv)
    d_raw = sum(advanced(d_conv, taps - 1 - k) * kernel[:, k] for k in range(taps))
    d_kernel = jnp.stack(
        [jnp.sum(delayed(raw, taps - 1 - k) * d_conv, axis=0) for k in range(taps)], axis=0
    )
    return d_raw, d_kernel


def pad_lanes(a):
    extra = -a.shape[-1] % LANES
    return a if extra == 0 else jnp.pad(a, ((0, 0),) * (a.ndim - 1) + ((0, extra),))


def as_rows(flat):
    return jnp.pad(flat, (0, -flat.shape[0] % (8 * LANES))).reshape(-1, LANES)


def on_device(
    block_in, cotangent, norm_gain, w_x, w_z, w_bc, w_dt, conv_x, conv_bc, dt_bias, a_log, skip,
    gate_gain, w_out,
):
    length, width = block_in.shape
    head_count, head_width, taps = conv_x.shape
    state = conv_bc.shape[1]
    inner = head_count * head_width
    heads, tensors, count = (lax.axis_size(a) for a in ("head", "tensor", "fsdp"))
    size = heads * tensors
    head_at = lax.axis_index("head")
    group_at = head_at * tensors + lax.axis_index("tensor")
    quarter = 2 * state // size
    rows = w_x.shape[0]
    owned = length // size
    full_inner = inner * size

    packed = jnp.concatenate(
        [
            w_x.reshape(rows, inner),
            w_z.reshape(rows, inner),
            w_bc.reshape(rows, 2 * state),
            pad_lanes(w_dt),
            w_out.reshape(inner, rows).T,
        ],
        axis=1,
    )
    weights = ring_gather(packed)
    dt_at = 2 * inner + 2 * state
    out_at = packed.shape[1] - inner
    weight_out = weights[:, out_at:]
    features = block_in.astype(jnp.float32)
    scale_in = lax.rsqrt(jnp.mean(features * features, axis=1, keepdims=True) + EPSILON)
    normed = (features * scale_in * norm_gain).astype(jnp.bfloat16)
    raw = jnp.dot(normed, weights[:, :out_at], preferred_element_type=jnp.float32)
    x_raw = raw[:, :inner]
    z_raw = raw[:, inner : 2 * inner]
    bc_raw = raw[:, 2 * inner : dt_at]
    dt_in = raw[:, dt_at : dt_at + head_count] + dt_bias
    kernel_x = conv_x.reshape(inner, taps)
    kernel_bc = conv_bc.reshape(2 * state, taps)
    gain = gate_gain.reshape(inner)
    x_conv = causal_conv(x_raw, kernel_x)
    x_act = jax.nn.silu(x_conv).astype(jnp.bfloat16)
    bc_act = jax.nn.silu(causal_conv(bc_raw, kernel_bc)).astype(jnp.bfloat16)
    b_maps, c_maps = bc_act[:, :state], bc_act[:, state:]

    per = max(1, LANES // head_width)
    step = jax.nn.softplus(dt_in)
    rate = -jnp.exp(a_log)
    at = jnp.arange(length)
    lower = (at[:, None] >= at[None, :]).astype(jnp.float32)
    cums = jnp.dot(lower, step * rate, precision=PRECISE)

    def as_columns(a):
        return a.reshape(length, head_count // per, per).transpose(1, 0, 2)

    def from_columns(a):
        return a.transpose(1, 0, 2).reshape(length, head_count)

    step_col = as_columns(step)
    col = as_columns(cums)
    row = cums.T.reshape(head_count // per, per, length)
    scanned = mix(b_maps, c_maps, x_act, step_col, col, row, head_width)
    skip_row = jnp.repeat(skip, head_width)[None, :]
    x_wide = x_act.astype(jnp.float32)
    mixed = scanned + skip_row * x_wide
    z_sigma = jax.nn.sigmoid(z_raw)
    z_silu = z_raw * z_sigma
    gated = mixed * z_silu
    d_normed_out = jnp.dot(cotangent, weight_out, preferred_element_type=jnp.float32)
    d_hat = d_normed_out * gain
    sums = jnp.concatenate([jnp.sum(gated * gated, axis=1), jnp.sum(d_hat * gated, axis=1)])
    sums = group_sum(sums.reshape(-1, LANES), False, 2).reshape(2, length)
    scale_out = lax.rsqrt(sums[0] / full_inner + EPSILON)[:, None]
    inner_sum = sums[1][:, None]
    normed_out = (gated * scale_out * gain).astype(jnp.bfloat16)
    partial_out = last_axes(normed_out, weight_out).astype(jnp.bfloat16)
    mine = lambda a: lax.dynamic_slice_in_dim(a, group_at * owned, owned, 0)
    g_gate_gain = jnp.sum(d_normed_out * gated * scale_out, axis=0)
    d_gated = scale_out * d_hat - gated * scale_out**3 * (inner_sum / full_inner)
    d_mixed = d_gated * z_silu
    d_z = (d_gated * mixed * (z_sigma * (1.0 + z_raw * (1.0 - z_sigma)))).astype(jnp.bfloat16)
    d_xs, d_step, d_cums, d_b, d_c = mix_back(
        b_maps, c_maps, x_act, d_mixed, scanned, skip_row, step_col, col, row, head_width
    )
    d_logs = jnp.dot(lower.T, from_columns(d_cums), precision=PRECISE)
    d_step = from_columns(d_step) + d_logs * rate
    d_dt_part = d_step * jax.nn.sigmoid(dt_in)
    g_a_log = jnp.sum(d_logs * step, axis=0) * rate
    g_skip = jnp.sum((d_mixed * x_wide).reshape(length, head_count, head_width), axis=(0, 2))

    d_bc_part = jnp.concatenate([d_b, d_c], axis=1)
    pieces = []
    for place in range(size):
        same = (head_at == place // tensors).astype(jnp.float32)
        pieces.append(
            pad_lanes(
                jnp.concatenate(
                    [d_bc_part[:, place * quarter : (place + 1) * quarter], d_dt_part * same], axis=1
                )
            )
        )
    d_small = group_sum(jnp.stack(pieces).astype(jnp.bfloat16), True, 5)
    d_bc = d_small[:, :quarter]
    d_dt = d_small[:, quarter : quarter + head_count]
    g_dt_bias = jnp.sum(d_dt, axis=0)

    own_cols = lambda a, axis: lax.dynamic_slice_in_dim(a, group_at * quarter, quarter, axis)
    bc_raw_own = own_cols(bc_raw, 1)
    kernel_bc_own = own_cols(kernel_bc, 0)
    d_bc_raw, g_conv_bc = conv_silu_back(
        bc_raw_own, causal_conv(bc_raw_own, kernel_bc_own), kernel_bc_own, d_bc
    )
    d_x_raw, g_conv_x = conv_silu_back(x_raw, x_conv, kernel_x, d_xs)
    d_cat = jnp.concatenate(
        [
            d_x_raw.astype(jnp.bfloat16),
            d_z,
            pad_lanes(jnp.concatenate([d_bc_raw, d_dt], axis=1).astype(jnp.bfloat16)),
        ],
        axis=1,
    )
    only = (lax.axis_index("tensor") == 0).astype(jnp.bfloat16)
    side = pad_lanes(
        jnp.concatenate(
            [own_cols(weights[:, 2 * inner : dt_at], 1), weights[:, dt_at : dt_at + head_count] * only],
            axis=1,
        )
    )
    local_part = last_axes(d_cat[:, : 2 * inner], weights[:, : 2 * inner]) + last_axes(
        d_cat[:, 2 * inner :], side
    )
    grads = jnp.concatenate(
        [
            first_axes(normed, d_cat).astype(jnp.bfloat16),
            first_axes(cotangent, normed_out).astype(jnp.bfloat16),
        ],
        axis=1,
    )
    lone = as_rows(jnp.concatenate([g_conv_x.reshape(-1), g_gate_gain, g_dt_bias]))
    spread = jnp.zeros((2 * state, taps), jnp.float32)
    spread = lax.dynamic_update_slice_in_dim(spread, g_conv_bc.T, group_at * quarter, 0)
    by_head = jnp.zeros((heads, 2 * head_count), jnp.float32)
    by_head = lax.dynamic_update_slice_in_dim(
        by_head, jnp.concatenate([g_a_log, g_skip])[None], head_at, 0
    )
    shared = as_rows(jnp.concatenate([spread.reshape(-1), by_head.reshape(-1)]))
    side_at = 2 * inner
    own, out_all, grad_all, bc_all, lone, shared, g_norm_gain = closing(
        grads.reshape(count, rows, grads.shape[1]),
        local_part.astype(jnp.bfloat16).reshape(size, owned, width),
        partial_out.reshape(size, owned, width),
        mine(features),
        mine(scale_in),
        norm_gain[None, :],
        lone,
        shared,
        side_at,
    )
    block_out = out_all.reshape(length, width)
    grad_in = grad_all.reshape(length, width).astype(jnp.float32) + cotangent.astype(jnp.float32)
    g_w_bc = bc_all[:, :, :quarter].transpose(1, 0, 2).reshape(rows, 2, state)
    lone, shared = lone.reshape(-1), shared.reshape(-1)
    at_heads = 2 * state * taps
    by_head = lax.dynamic_slice_in_dim(
        shared[at_heads : at_heads + 2 * head_count * heads].reshape(heads, 2 * head_count), head_at, 1, 0
    )[0]
    wide = taps * inner
    return (
        block_out,
        grad_in,
        g_norm_gain.reshape(width),
        own[:, :inner].reshape(rows, head_count, head_width),
        own[:, inner : 2 * inner].reshape(rows, head_count, head_width),
        g_w_bc,
        own[:, side_at + quarter : side_at + quarter + head_count],
        lone[:wide].reshape(taps, inner).T.reshape(head_count, head_width, taps),
        shared[:at_heads].reshape(2, state, taps),
        lone[wide + inner : wide + inner + head_count],
        by_head[:head_count],
        by_head[head_count:],
        lone[wide : wide + inner].reshape(head_count, head_width),
        own[:, own.shape[1] - inner :].T.reshape(head_count, head_width, rows),
    )


def solution(mesh):
    return jax.shard_map(
        on_device,
        mesh=mesh,
        in_specs=(
            P("fsdp", None),
            P("fsdp", None),
            P(),
            P("fsdp", "head", "tensor"),
            P("fsdp", "head", "tensor"),
            P("fsdp", None, None),
            P("fsdp", "head"),
            P("head", "tensor", None),
            P(),
            P("head"),
            P("head"),
            P("head"),
            P("head", "tensor"),
            P("head", "tensor", "fsdp"),
        ),
        out_specs=(
            P("fsdp", None),
            P("fsdp", None),
            P(),
            P("fsdp", "head", "tensor"),
            P("fsdp", "head", "tensor"),
            P("fsdp", None, None),
            P("fsdp", "head"),
            P("head", "tensor", None),
            P(),
            P("head"),
            P("head"),
            P("head"),
            P("head", "tensor"),
            P("head", "tensor", "fsdp"),
        ),
        check_vma=False,
    )
```

```python
from functools import partial

import jax
import jax.numpy as jnp
from jax import lax
from jax.experimental import pallas as pl
from jax.experimental.pallas import tpu as pltpu
from jax.sharding import PartitionSpec as P

EPSILON = 1e-05
PRECISE = lax.Precision.HIGHEST
LANES = 128
CHUNK = 256
WAYS = 6
MESH = pl.DeviceIdType.MESH
VMEM_SPEC = pl.BlockSpec(memory_space=pltpu.VMEM)


def ring_index(position, count):
    high = position // (count // 2)
    return (1 - high) * 2 * position + high * (2 * (count - 1 - position) + 1)


def ring_position(index, count):
    odd = index % 2
    return (1 - odd) * (index // 2) + odd * (count - 1 - index // 2)


def ring_setup(count):
    me = lax.axis_index("fsdp")
    position = ring_position(me, count)
    right = ring_index((position + 1) % count, count)
    left = ring_index((position + count - 1) % count, count)
    barrier = pltpu.get_barrier_semaphore()
    for neighbour in (left, right):
        pl.semaphore_signal(barrier, inc=1, device_id={"fsdp": neighbour}, device_id_type=MESH)
    pl.semaphore_wait(barrier, 2)
    return me, position, (right, left)


def column_ways(width):
    tiles = width // LANES
    share, extra = tiles // WAYS, tiles % WAYS
    cuts, start = [], 0
    for way in range(WAYS):
        amount = (share + (1 if way < extra else 0)) * LANES
        cuts.append((start, amount))
        start += amount
    return cuts


def gather_kernel(count, x_ref, o_ref, local_sem, send_sem, recv_sem):
    me, position, targets = ring_setup(count)
    local = pltpu.make_async_copy(x_ref, o_ref.at[me], local_sem)
    local.start()
    ways = column_ways(x_ref.shape[1])
    copies = [[] for _ in ways]
    for step in range(count - 1):
        for way, (start, amount) in enumerate(ways):
            shift = count - step if way % 2 == 0 else step
            block = ring_index((position + shift) % count, count)
            columns = pl.ds(start, amount)
            target = o_ref.at[block, :, columns]
            source = x_ref.at[:, columns] if step == 0 else target
            if step > 0:
                copies[way][step - 1].wait_recv()
            copy = pltpu.make_async_remote_copy(
                src_ref=source,
                dst_ref=target,
                send_sem=send_sem.at[way, step],
                recv_sem=recv_sem.at[way, step],
                device_id={"fsdp": targets[way % 2]},
                device_id_type=MESH,
            )
            copy.start()
            copies[way].append(copy)
    for way in range(len(ways)):
        copies[way][count - 2].wait_recv()
        for copy in copies[way]:
            copy.wait_send()
    local.wait()


def ring_gather(shard):
    count = lax.axis_size("fsdp")
    rows, width = shard.shape
    return pl.pallas_call(
        partial(gather_kernel, count),
        out_shape=jax.ShapeDtypeStruct((count, rows, width), shard.dtype),
        in_specs=[VMEM_SPEC],
        out_specs=pl.BlockSpec(memory_space=pl.ANY),
        scratch_shapes=[
            pltpu.SemaphoreType.DMA,
            pltpu.SemaphoreType.DMA((WAYS, count - 1)),
            pltpu.SemaphoreType.DMA((WAYS, count - 1)),
        ],
        compiler_params=pltpu.CompilerParams(collective_id=0, has_side_effects=True),
        name="ring_gather",
    )(shard).reshape(count * rows, width)


def send(source, target, sems, place, device):
    copy = pltpu.make_async_remote_copy(
        src_ref=source,
        dst_ref=target,
        send_sem=sems[0].at[place],
        recv_sem=sems[1].at[place],
        device_id=device,
        device_id_type=MESH,
    )
    copy.start()
    return copy


def closing_kernel(
    count, heads, tensors, side_at,
    g_ref, dn_ref, po_ref, feat_ref, scale_ref, gain_ref, lone_ref, shared_ref,
    own_ref, out_ref, grad_ref, bc_ref, lone_out, shared_out, norm_out,
    *scratch,
):
    slots = scratch[:WAYS]
    (held_a, stage, held_b, norm_own, norm_held, norm_sum, shared_held, shared_sum,
     lone_all, shared_all, norm_all) = scratch[WAYS : WAYS + 11]
    sem = scratch[WAYS + 11 :]
    pairs = [(sem[2 * i], sem[2 * i + 1]) for i in range(len(sem) // 2)]
    ring_sems, a_sems, b_sems, at_sems, ah_sems, group_sems, lone_sems, late_sems, bc_sems = pairs
    me = lax.axis_index("fsdp")
    position = ring_position(me, count)
    targets = (
        ring_index((position + 1) % count, count),
        ring_index((position + count - 1) % count, count),
    )
    group_me, peers = group_peers(heads, tensors)
    head, tensor = lax.axis_index("head"), lax.axis_index("tensor")
    others = [(me + offset) % count for offset in range(1, count)]
    barrier = pltpu.get_barrier_semaphore()
    for h, t in peers:
        pl.semaphore_signal(barrier, inc=1, device_id={"head": h, "tensor": t}, device_id_type=MESH)
    for other in others:
        pl.semaphore_signal(barrier, inc=1, device_id={"fsdp": other}, device_id_type=MESH)
    pl.semaphore_wait(barrier, len(peers) + len(others))

    started = []

    def sent(*args):
        copy = send(*args)
        started.append(copy)
        return copy

    head_peers = [(head + offset) % heads for offset in range(1, heads)]
    tensor_peers = [(tensor + offset) % tensors for offset in range(1, tensors)]
    parts = (dn_ref, po_ref)
    results = (grad_ref, out_ref)
    phase = {}

    def start_a():
        for i, ref in enumerate(parts):
            phase["a", i] = [
                sent(
                    ref.at[pl.ds(peer * tensors, tensors)], held_a.at[i, k], a_sems, (i, k),
                    {"head": peer},
                )
                for k, peer in enumerate(head_peers)
            ]
        phase["lone"] = [
            sent(lone_ref, lone_all.at[me], lone_sems, k, {"fsdp": other})
            for k, other in enumerate(others)
        ]
        lone_all[me] = lone_ref[...]

    def to_b(i):
        for copy in phase["a", i]:
            copy.wait_recv()
        for t in range(tensors):
            total = parts[i][head * tensors + t].astype(jnp.float32)
            for k in range(heads - 1):
                total = total + held_a[i, k, t].astype(jnp.float32)
            stage[i, t] = total.astype(stage.dtype)
        phase["b", i] = [
            sent(stage.at[i, peer], held_b.at[i, k], b_sems, (i, k), {"tensor": peer})
            for k, peer in enumerate(tensor_peers)
        ]

    def spread(i):
        for copy in phase["b", i]:
            copy.wait_recv()
        total = stage[i, tensor].astype(jnp.float32)
        for k in range(tensors - 1):
            total = total + held_b[i, k].astype(jnp.float32)
        features = feat_ref[...]
        if i == 0:
            scale = scale_ref[...]
            norm_own[...] = jnp.sum(total * (features * scale), axis=0, keepdims=True)
            inner = total * gain_ref[...]
            mean = jnp.mean(inner * features, axis=1, keepdims=True)
            value = scale * inner - features * (scale * scale * scale * mean)
        else:
            value = total + features
        result = results[i]
        result[group_me] = value.astype(result.dtype)
        mine = result.at[group_me]
        phase["t", i] = [
            sent(mine, mine, at_sems, (i, k), {"tensor": peer}) for k, peer in enumerate(tensor_peers)
        ]
        phase["h", i] = [
            sent(mine, mine, ah_sems, (i, k, 0), {"head": peer}) for k, peer in enumerate(head_peers)
        ]
        if i == 0:
            norm_held[group_me] = norm_own[...]
            shared_held[group_me] = shared_ref[...]
            phase["group"] = []
            for k, (h, t) in enumerate(peers):
                device = {"head": h, "tensor": t}
                phase["group"] += [
                    sent(norm_own, norm_held.at[group_me], group_sems, (0, k), device),
                    sent(shared_ref, shared_held.at[group_me], group_sems, (1, k), device),
                ]

    def forward(i):
        result = results[i]
        for k, copy in enumerate(phase["t", i]):
            copy.wait_recv()
            block = result.at[head * tensors + (tensor + tensors - 1 - k) % tensors]
            phase["h", i] += [
                sent(block, block, ah_sems, (i, j, k + 1), {"head": peer})
                for j, peer in enumerate(head_peers)
            ]

    def late():
        for copy in phase["group"]:
            copy.wait_recv()
        for held, total, everyone, place in (
            (norm_held, norm_sum, norm_all, 0),
            (shared_held, shared_sum, shared_all, 1),
        ):
            value = held[0]
            for k in range(1, heads * tensors):
                value = value + held[k]
            total[...] = value
            everyone[me] = value
            phase["late", place] = [
                sent(total, everyone.at[me], late_sems, (place, k), {"fsdp": other})
                for k, other in enumerate(others)
            ]

    events = [
        (0, start_a),
        (1, lambda: to_b(0)), (1, lambda: to_b(1)),
        (2, lambda: spread(0)), (3, lambda: spread(1)),
        (4, lambda: forward(0)), (4, late), (5, lambda: forward(1)),
    ]
    ways = column_ways(g_ref.shape[2])
    ring = [[] for _ in ways]
    for step in range(count - 1):
        for way, (start, amount) in enumerate(ways):
            columns = pl.ds(start, amount)
            shift = 2 * count - 1 - step if way % 2 == 0 else 1 + step
            block = ring_index((position + shift) % count, count)
            held = slots[way]
            if step == 0:
                source = g_ref.at[block, :, columns]
            else:
                ring[way][step - 1].wait_recv()
                held[step - 1] = (
                    held[step - 1].astype(jnp.float32)
                    + g_ref[block, :, columns].astype(jnp.float32)
                ).astype(held.dtype)
                source = held.at[step - 1]
            ring[way].append(
                sent(source, held.at[step], ring_sems, (way, step), {"fsdp": targets[way % 2]})
            )
        while events and events[0][0] <= step:
            events.pop(0)[1]()
    for _, event in events:
        event()
    side = pl.ds(side_at, LANES)
    order = sorted(
        range(len(ways)), key=lambda way: not ways[way][0] <= side_at < ways[way][0] + ways[way][1]
    )
    for way in order:
        start, amount = ways[way]
        columns = pl.ds(start, amount)
        ring[way][count - 2].wait_recv()
        own_ref[:, columns] = slots[way][count - 2].astype(jnp.float32) + g_ref[
            me, :, columns
        ].astype(jnp.float32)
        if start <= side_at < start + amount:
            bc_ref[group_me] = own_ref[:, side]
            bc_copies = [
                sent(bc_ref.at[group_me], bc_ref.at[group_me], bc_sems, k, {"head": h, "tensor": t})
                for k, (h, t) in enumerate(peers)
            ]
    for copies, everyone, total in (
        (phase["lone"], lone_all, lone_out),
        (phase["late", 0], norm_all, norm_out),
        (phase["late", 1], shared_all, shared_out),
    ):
        for copy in copies:
            copy.wait_recv()
        value = everyone[0]
        for k in range(1, count):
            value = value + everyone[k]
        total[...] = value
    for i in range(2):
        for copy in phase["h", i]:
            copy.wait_recv()
    for copy in bc_copies:
        copy.wait_recv()
    for copy in started:
        copy.wait_send()


def closing(grads, d_normed, partial_out, features, scale, gain, lone, shared, side_at):
    count, heads, tensors = (lax.axis_size(a) for a in ("fsdp", "head", "tensor"))
    size = heads * tensors
    _, rows, columns = grads.shape
    _, owned, width = d_normed.shape
    low, full = grads.dtype, jnp.float32
    ways = column_ways(columns)
    assert all(amount > 0 for _, amount in ways)
    dma = pltpu.SemaphoreType.DMA
    shapes = [
        (WAYS, count - 1), (2, heads - 1), (2, tensors - 1), (2, tensors - 1),
        (2, heads - 1, tensors), (2, size - 1), (count - 1,), (2, count - 1), (size - 1,),
    ]
    return pl.pallas_call(
        partial(closing_kernel, count, heads, tensors, side_at),
        out_shape=[
            jax.ShapeDtypeStruct((rows, columns), full),
            jax.ShapeDtypeStruct((size, owned, width), low),
            jax.ShapeDtypeStruct((size, owned, width), low),
            jax.ShapeDtypeStruct((size, rows, LANES), full),
            jax.ShapeDtypeStruct(lone.shape, full),
            jax.ShapeDtypeStruct(shared.shape, full),
            jax.ShapeDtypeStruct((1, width), full),
        ],
        in_specs=[VMEM_SPEC] * 8,
        out_specs=[VMEM_SPEC] * 7,
        scratch_shapes=[pltpu.VMEM((count - 1, rows, amount), low) for _, amount in ways]
        + [
            pltpu.VMEM((2, heads - 1, tensors, owned, width), low),
            pltpu.VMEM((2, tensors, owned, width), low),
            pltpu.VMEM((2, tensors - 1, owned, width), low),
            pltpu.VMEM((1, width), full),
            pltpu.VMEM((size, 1, width), full),
            pltpu.VMEM((1, width), full),
            pltpu.VMEM((size,) + shared.shape, full),
            pltpu.VMEM(shared.shape, full),
            pltpu.VMEM((count,) + lone.shape, full),
            pltpu.VMEM((count,) + shared.shape, full),
            pltpu.VMEM((count, 1, width), full),
        ]
        + [dma(shape) for shape in shapes for _ in range(2)],
        compiler_params=pltpu.CompilerParams(collective_id=1, has_side_effects=True),
        name="closing",
    )(grads, d_normed, partial_out, features, scale, gain, lone, shared)


def group_peers(heads, tensors):
    head, tensor = lax.axis_index("head"), lax.axis_index("tensor")
    peers = []
    for offset in range(1, heads * tensors):
        peer_head = (head + offset // tensors) % heads
        peer_tensor = (tensor + offset % tensors) % tensors
        peers.append((peer_head, peer_tensor))
    return head * tensors + tensor, peers


def group_barrier(peers):
    barrier = pltpu.get_barrier_semaphore()
    for head, tensor in peers:
        pl.semaphore_signal(
            barrier, inc=1, device_id={"head": head, "tensor": tensor}, device_id_type=MESH
        )
    pl.semaphore_wait(barrier, len(peers))


def group_exchange(peers, source_of, target, send_sem, recv_sem):
    copies = []
    for place, (head, tensor) in enumerate(peers):
        copy = pltpu.make_async_remote_copy(
            src_ref=source_of(head, tensor),
            dst_ref=target,
            send_sem=send_sem.at[place],
            recv_sem=recv_sem.at[place],
            device_id={"head": head, "tensor": tensor},
            device_id_type=MESH,
        )
        copy.start()
        copies.append(copy)
    return copies


def group_sum_kernel(heads, tensors, scattered, x_ref, o_ref, held, send_sem, recv_sem):
    me, peers = group_peers(heads, tensors)
    group_barrier(peers)

    def source_of(head, tensor):
        return x_ref.at[head * tensors + tensor] if scattered else x_ref

    copies = group_exchange(peers, source_of, held.at[me], send_sem, recv_sem)
    held[me] = x_ref[me] if scattered else x_ref[...]
    for copy in copies:
        copy.wait_recv()
    total = held[0].astype(jnp.float32)
    for place in range(1, heads * tensors):
        total = total + held[place].astype(jnp.float32)
    o_ref[...] = total
    for copy in copies:
        copy.wait_send()


def group_sum(x, scattered, collective):
    heads, tensors = lax.axis_size("head"), lax.axis_size("tensor")
    size = heads * tensors
    shape = x.shape[1:] if scattered else x.shape
    return pl.pallas_call(
        partial(group_sum_kernel, heads, tensors, scattered),
        out_shape=jax.ShapeDtypeStruct(shape, jnp.float32),
        in_specs=[VMEM_SPEC],
        out_specs=VMEM_SPEC,
        scratch_shapes=[
            pltpu.VMEM((size,) + shape, x.dtype),
            pltpu.SemaphoreType.DMA((size - 1,)),
            pltpu.SemaphoreType.DMA((size - 1,)),
        ],
        compiler_params=pltpu.CompilerParams(collective_id=collective, has_side_effects=True),
        name=f"group_sum_{collective}",
    )(x)


def decay_tile(cums_col, cums_row, first_row, rows, columns):
    gap = cums_col - cums_row
    row = first_row + lax.broadcasted_iota(jnp.int32, (rows, columns), 0)
    column = lax.broadcasted_iota(jnp.int32, (rows, columns), 1)
    return jnp.exp(jnp.where(row >= column, gap, -1e30))


def last_axes(a, b):
    return lax.dot_general(a, b, (((1,), (1,)), ((), ())), preferred_element_type=jnp.float32)


def first_axes(a, b):
    return lax.dot_general(a, b, (((0,), (0,)), ((), ())), preferred_element_type=jnp.float32)


def mix_kernel(per, width, b_ref, c_ref, x_ref, row_ref, y_ref, scores):
    length = x_ref.shape[0]
    chunk = min(CHUNK, length)

    @pl.when(pl.program_id(0) == 0)
    def _():
        scores[...] = last_axes(c_ref[...], b_ref[...])

    columns = row_ref[0].T
    for head in range(per):
        part = slice(head * width, (head + 1) * width)
        step = columns[:, head : head + 1]
        v = (x_ref[:, part].astype(jnp.float32) * step).astype(jnp.bfloat16)
        for first in range(0, length, chunk):
            seen = first + chunk
            decay = decay_tile(
                columns[first:seen, per + head : per + head + 1],
                row_ref[0, per + head : per + head + 1, :seen],
                first,
                chunk,
                seen,
            )
            a = (scores[first:seen, :seen] * decay).astype(jnp.bfloat16)
            y_ref[first:seen, part] = jnp.dot(a, v[:seen], preferred_element_type=jnp.float32)


def back_kernel(
    per, width, b_ref, c_ref, x_ref, dy_ref, y_ref, skip_ref, row_ref,
    dx_ref, drow_ref, db_ref, dc_ref, scores, d_scores, carried, side, low_v, low_dy,
):
    length = x_ref.shape[0]
    chunk = min(CHUNK, length)

    @pl.when(pl.program_id(0) == 0)
    def _():
        scores[...] = last_axes(c_ref[...], b_ref[...])
        d_scores[...] = jnp.zeros_like(d_scores)

    columns = row_ref[0].T
    for head in range(per):
        part = slice(head * width, (head + 1) * width)
        step = columns[:, head : head + 1]
        x = x_ref[:, part].astype(jnp.float32)
        v = (x * step).astype(jnp.bfloat16)
        dy_low = dy_ref[:, part].astype(jnp.bfloat16)
        low_v[:, part] = v
        low_dy[:, part] = dy_low
        carried[part] = jnp.zeros((width, length), jnp.float32)
        for first in range(0, length, chunk):
            seen = first + chunk
            decay = decay_tile(
                columns[first:seen, per + head : per + head + 1],
                row_ref[0, per + head : per + head + 1, :seen],
                first,
                chunk,
                seen,
            )
            a = (scores[first:seen, :seen] * decay).astype(jnp.bfloat16)
            carried[part, :seen] += first_axes(dy_low[first:seen], a)
            d_scores[first:seen, :seen] += last_axes(dy_low[first:seen], v[:seen]) * decay

    u_all = carried[...].T
    for head in range(per):
        part = slice(head * width, (head + 1) * width)
        step = columns[:, head : head + 1]
        x = x_ref[:, part].astype(jnp.float32)
        v = low_v[:, part].astype(jnp.float32)
        dy_low = low_dy[:, part].astype(jnp.float32)
        u = u_all[:, part]
        dx_ref[:, part] = step * u + skip_ref[:, part] * dy_ref[:, part]
        side[:, head : head + 1] = jnp.sum(x * u, axis=1, keepdims=True)
        side[:, per + head : per + head + 1] = jnp.sum(
            dy_low * y_ref[:, part] - v * u, axis=1, keepdims=True
        )
    drow_ref[0] = side[...].T[: 2 * per]

    @pl.when(pl.program_id(0) == pl.num_programs(0) - 1)
    def _():
        low = d_scores[...].astype(jnp.bfloat16)
        dc_ref[...] = jnp.dot(low, b_ref[...], preferred_element_type=jnp.float32)
        db_ref[...] = first_axes(low, c_ref[...])


def whole(shape):
    return pl.BlockSpec(shape, lambda i: (0,) * len(shape))


def head_specs(length, per, width, state):
    wide = pl.BlockSpec((length, per * width), lambda i: (0, i))
    row = pl.BlockSpec((1, 2 * per, length), lambda i: (i, 0, 0))
    return whole((length, state)), wide, row


def mix(b, c, x, row, width):
    length, inner = x.shape
    per = row.shape[1] // 2
    maps, wide, row_spec = head_specs(length, per, width, b.shape[1])
    return pl.pallas_call(
        partial(mix_kernel, per, width),
        grid=(inner // (per * width),),
        in_specs=[maps, maps, wide, row_spec],
        out_specs=wide,
        out_shape=jax.ShapeDtypeStruct((length, inner), jnp.float32),
        scratch_shapes=[pltpu.VMEM((length, length), jnp.float32)],
        name="mix",
    )(b, c, x, row)


def mix_back(b, c, x, dy, y, skip_row, row, width):
    length, inner = x.shape
    groups, per = row.shape[0], row.shape[1] // 2
    state = b.shape[1]
    maps, wide, row_spec = head_specs(length, per, width, state)
    return pl.pallas_call(
        partial(back_kernel, per, width),
        grid=(groups,),
        in_specs=[
            maps, maps, wide, wide, wide,
            pl.BlockSpec((1, per * width), lambda i: (0, i)),
            row_spec,
        ],
        out_specs=[wide, row_spec, maps, maps],
        out_shape=[
            jax.ShapeDtypeStruct((length, inner), jnp.float32),
            jax.ShapeDtypeStruct(row.shape, jnp.float32),
            jax.ShapeDtypeStruct((length, state), jnp.float32),
            jax.ShapeDtypeStruct((length, state), jnp.float32),
        ],
        scratch_shapes=[
            pltpu.VMEM((length, length), jnp.float32),
            pltpu.VMEM((length, length), jnp.float32),
            pltpu.VMEM((per * width, length), jnp.float32),
            pltpu.VMEM((length, LANES), jnp.float32),
            pltpu.VMEM((length, per * width), jnp.bfloat16),
            pltpu.VMEM((length, per * width), jnp.bfloat16),
        ],
        name="mix_back",
    )(b, c, x, dy, y, skip_row, row)


def delayed(signal, count):
    return signal if count == 0 else jnp.pad(signal, ((count, 0), (0, 0)))[: signal.shape[0]]


def advanced(signal, count):
    return signal if count == 0 else jnp.pad(signal, ((0, count), (0, 0)))[count:]


def causal_conv(signal, kernel):
    taps = kernel.shape[1]
    return sum(delayed(signal, taps - 1 - k) * kernel[:, k] for k in range(taps))


def silu_slope(value):
    sigma = jax.nn.sigmoid(value)
    return sigma * (1.0 + value * (1.0 - sigma))


def conv_silu_back(raw, conv, kernel, upstream):
    taps = kernel.shape[1]
    d_conv = upstream * silu_slope(conv)
    d_raw = sum(advanced(d_conv, taps - 1 - k) * kernel[:, k] for k in range(taps))
    d_kernel = jnp.stack(
        [jnp.sum(delayed(raw, taps - 1 - k) * d_conv, axis=0) for k in range(taps)], axis=0
    )
    return d_raw, d_kernel


def pad_lanes(a):
    extra = -a.shape[-1] % LANES
    return a if extra == 0 else jnp.pad(a, ((0, 0),) * (a.ndim - 1) + ((0, extra),))


def as_rows(flat):
    return jnp.pad(flat, (0, -flat.shape[0] % (8 * LANES))).reshape(-1, LANES)


def on_device(
    block_in, cotangent, norm_gain, w_x, w_z, w_bc, w_dt, conv_x, conv_bc, dt_bias, a_log, skip,
    gate_gain, w_out,
):
    length, width = block_in.shape
    head_count, head_width, taps = conv_x.shape
    state = conv_bc.shape[1]
    inner = head_count * head_width
    heads, tensors, count = (lax.axis_size(a) for a in ("head", "tensor", "fsdp"))
    size = heads * tensors
    head_at = lax.axis_index("head")
    group_at = head_at * tensors + lax.axis_index("tensor")
    quarter = 2 * state // size
    rows = w_x.shape[0]
    owned = length // size
    full_inner = inner * size

    packed = jnp.concatenate(
        [
            w_x.reshape(rows, inner),
            w_z.reshape(rows, inner),
            w_bc.reshape(rows, 2 * state),
            pad_lanes(w_dt),
            w_out.reshape(inner, rows).T,
        ],
        axis=1,
    )
    weights = ring_gather(packed)
    dt_at = 2 * inner + 2 * state
    out_at = packed.shape[1] - inner
    weight_out = weights[:, out_at:]
    features = block_in.astype(jnp.float32)
    scale_in = lax.rsqrt(jnp.mean(features * features, axis=1, keepdims=True) + EPSILON)
    normed = (features * scale_in * norm_gain).astype(jnp.bfloat16)
    raw = jnp.dot(normed, weights[:, :out_at], preferred_element_type=jnp.float32)
    x_raw = raw[:, :inner]
    z_raw = raw[:, inner : 2 * inner]
    bc_raw = raw[:, 2 * inner : dt_at]
    dt_in = raw[:, dt_at : dt_at + head_count].T + dt_bias[:, None]
    kernel_x = conv_x.reshape(inner, taps)
    kernel_bc = conv_bc.reshape(2 * state, taps)
    gain = gate_gain.reshape(inner)
    x_conv = causal_conv(x_raw, kernel_x)
    x_act = jax.nn.silu(x_conv).astype(jnp.bfloat16)
    bc_act = jax.nn.silu(causal_conv(bc_raw, kernel_bc)).astype(jnp.bfloat16)
    b_maps, c_maps = bc_act[:, :state], bc_act[:, state:]

    per = max(1, LANES // head_width)
    step = jax.nn.softplus(dt_in)
    rate = -jnp.exp(a_log)
    at = jnp.arange(length)
    lower = (at[:, None] >= at[None, :]).astype(jnp.float32)
    cums = jnp.dot(step * rate[:, None], lower.T, precision=PRECISE)
    by_group = (head_count // per, per, length)
    row = jnp.concatenate([step.reshape(by_group), cums.reshape(by_group)], axis=1)
    scanned = mix(b_maps, c_maps, x_act, row, head_width)
    skip_row = jnp.repeat(skip, head_width)[None, :]
    x_wide = x_act.astype(jnp.float32)
    mixed = scanned + skip_row * x_wide
    z_sigma = jax.nn.sigmoid(z_raw)
    z_silu = z_raw * z_sigma
    gated = mixed * z_silu
    d_normed_out = jnp.dot(cotangent, weight_out, preferred_element_type=jnp.float32)
    d_hat = d_normed_out * gain
    sums = jnp.concatenate([jnp.sum(gated * gated, axis=1), jnp.sum(d_hat * gated, axis=1)])
    sums = group_sum(sums.reshape(-1, LANES), False, 2).reshape(2, length)
    scale_out = lax.rsqrt(sums[0] / full_inner + EPSILON)[:, None]
    inner_sum = sums[1][:, None]
    normed_out = (gated * scale_out * gain).astype(jnp.bfloat16)
    partial_out = last_axes(normed_out, weight_out).astype(jnp.bfloat16)
    mine = lambda a: lax.dynamic_slice_in_dim(a, group_at * owned, owned, 0)
    g_gate_gain = jnp.sum(d_normed_out * gated * scale_out, axis=0)
    d_gated = scale_out * d_hat - gated * scale_out**3 * (inner_sum / full_inner)
    d_mixed = d_gated * z_silu
    d_z = (d_gated * mixed * (z_sigma * (1.0 + z_raw * (1.0 - z_sigma)))).astype(jnp.bfloat16)
    d_xs, d_row, d_b, d_c = mix_back(
        b_maps, c_maps, x_act, d_mixed, scanned, skip_row, row, head_width
    )
    d_logs = jnp.dot(d_row[:, per:].reshape(head_count, length), lower, precision=PRECISE)
    d_step = d_row[:, :per].reshape(head_count, length) + d_logs * rate[:, None]
    d_dt_part = (d_step * jax.nn.sigmoid(dt_in)).T
    g_a_log = jnp.sum(d_logs * step, axis=1) * rate
    g_skip = jnp.sum((d_mixed * x_wide).reshape(length, head_count, head_width), axis=(0, 2))

    d_bc_part = jnp.concatenate([d_b, d_c], axis=1)
    pieces = []
    for place in range(size):
        same = (head_at == place // tensors).astype(jnp.float32)
        pieces.append(
            pad_lanes(
                jnp.concatenate(
                    [d_bc_part[:, place * quarter : (place + 1) * quarter], d_dt_part * same], axis=1
                )
            )
        )
    d_small = group_sum(jnp.stack(pieces).astype(jnp.bfloat16), True, 5)
    d_bc = d_small[:, :quarter]
    d_dt = d_small[:, quarter : quarter + head_count]
    g_dt_bias = jnp.sum(d_dt, axis=0)

    own_cols = lambda a, axis: lax.dynamic_slice_in_dim(a, group_at * quarter, quarter, axis)
    bc_raw_own = own_cols(bc_raw, 1)
    kernel_bc_own = own_cols(kernel_bc, 0)
    d_bc_raw, g_conv_bc = conv_silu_back(
        bc_raw_own, causal_conv(bc_raw_own, kernel_bc_own), kernel_bc_own, d_bc
    )
    d_x_raw, g_conv_x = conv_silu_back(x_raw, x_conv, kernel_x, d_xs)
    d_cat = jnp.concatenate(
        [
            d_x_raw.astype(jnp.bfloat16),
            d_z,
            pad_lanes(jnp.concatenate([d_bc_raw, d_dt], axis=1).astype(jnp.bfloat16)),
        ],
        axis=1,
    )
    only = (lax.axis_index("tensor") == 0).astype(jnp.bfloat16)
    side = pad_lanes(
        jnp.concatenate(
            [own_cols(weights[:, 2 * inner : dt_at], 1), weights[:, dt_at : dt_at + head_count] * only],
            axis=1,
        )
    )
    local_part = last_axes(d_cat[:, : 2 * inner], weights[:, : 2 * inner]) + last_axes(
        d_cat[:, 2 * inner :], side
    )
    grads = jnp.concatenate(
        [
            first_axes(normed, d_cat).astype(jnp.bfloat16),
            first_axes(cotangent, normed_out).astype(jnp.bfloat16),
        ],
        axis=1,
    )
    lone = as_rows(jnp.concatenate([g_conv_x.reshape(-1), g_gate_gain, g_dt_bias]))
    spread = jnp.zeros((2 * state, taps), jnp.float32)
    spread = lax.dynamic_update_slice_in_dim(spread, g_conv_bc.T, group_at * quarter, 0)
    by_head = jnp.zeros((heads, 2 * head_count), jnp.float32)
    by_head = lax.dynamic_update_slice_in_dim(
        by_head, jnp.concatenate([g_a_log, g_skip])[None], head_at, 0
    )
    shared = as_rows(jnp.concatenate([spread.reshape(-1), by_head.reshape(-1)]))
    side_at = 2 * inner
    own, out_all, grad_all, bc_all, lone, shared, g_norm_gain = closing(
        grads.reshape(count, rows, grads.shape[1]),
        local_part.astype(jnp.bfloat16).reshape(size, owned, width),
        partial_out.reshape(size, owned, width),
        mine(features),
        mine(scale_in),
        norm_gain[None, :],
        lone,
        shared,
        side_at,
    )
    block_out = out_all.reshape(length, width)
    grad_in = grad_all.reshape(length, width).astype(jnp.float32) + cotangent.astype(jnp.float32)
    g_w_bc = bc_all[:, :, :quarter].transpose(1, 0, 2).reshape(rows, 2, state)
    lone, shared = lone.reshape(-1), shared.reshape(-1)
    at_heads = 2 * state * taps
    by_head = lax.dynamic_slice_in_dim(
        shared[at_heads : at_heads + 2 * head_count * heads].reshape(heads, 2 * head_count), head_at, 1, 0
    )[0]
    wide = taps * inner
    return (
        block_out,
        grad_in,
        g_norm_gain.reshape(width),
        own[:, :inner].reshape(rows, head_count, head_width),
        own[:, inner : 2 * inner].reshape(rows, head_count, head_width),
        g_w_bc,
        own[:, side_at + quarter : side_at + quarter + head_count],
        lone[:wide].reshape(taps, inner).T.reshape(head_count, head_width, taps),
        shared[:at_heads].reshape(2, state, taps),
        lone[wide + inner : wide + inner + head_count],
        by_head[:head_count],
        by_head[head_count:],
        lone[wide : wide + inner].reshape(head_count, head_width),
        own[:, own.shape[1] - inner :].T.reshape(head_count, head_width, rows),
    )


def solution(mesh):
    return jax.shard_map(
        on_device,
        mesh=mesh,
        in_specs=(
            P("fsdp", None),
            P("fsdp", None),
            P(),
            P("fsdp", "head", "tensor"),
            P("fsdp", "head", "tensor"),
            P("fsdp", None, None),
            P("fsdp", "head"),
            P("head", "tensor", None),
            P(),
            P("head"),
            P("head"),
            P("head"),
            P("head", "tensor"),
            P("head", "tensor", "fsdp"),
        ),
        out_specs=(
            P("fsdp", None),
            P("fsdp", None),
            P(),
            P("fsdp", "head", "tensor"),
            P("fsdp", "head", "tensor"),
            P("fsdp", None, None),
            P("fsdp", "head"),
            P("head", "tensor", None),
            P(),
            P("head"),
            P("head"),
            P("head"),
            P("head", "tensor"),
            P("head", "tensor", "fsdp"),
        ),
        check_vma=False,
    )
```
